512 devices in a mesh: dp: 128 (over x, z, core), mp: 4 (over y).
Axes of the slice: x: 4, y: 4, z: 16, core: 2. Of those that a mesh axis runs over, the one named last changes fastest.
Arguments:
- media: bfloat16 [1024, 256, 1536], P('dp', None, 'mp'), may hold values from -24 to 24
- time_table: bfloat16 [8, 1536], P(None, 'mp'), may hold values from -4 to 4
- doc_images: int32 [256], P('dp'), may hold values from 0 to 8, as said below
- plan: int32 [128, 8], P('dp'), may hold values from -1 to 19, as said below
- latents: bfloat16 [64, 1536], replicated, may hold values from -6 to 6
- queries: bfloat16 [64, 1024], P(None, 'mp'), may hold values from -450 to 450
- key_weight: bfloat16 [1536, 1024], P(None, 'mp'), may hold values from -0.15625 to 0.15625
- value_weight: bfloat16 [1536, 1024], P(None, 'mp'), may hold values from -0.15625 to 0.15625
- out_weight: bfloat16 [1024, 1536], P('mp'), may hold values from -0.1875 to 0.1875
- cotangent: bfloat16 [512, 64, 1536], P('dp', None, 'mp'), may hold values from -6 to 6
Outputs:
- resampled: bfloat16 [512, 64, 1536], P('dp', None, 'mp')
- key_grad: float32 [1536, 1024], P('dp', 'mp')
- value_grad: float32 [1536, 1024], P('dp', 'mp')
The draws below stay inside these ranges and needn't reach their ends.
Inputs may be any that keep to these rules, and one draw needn't show every extreme that they name: `doc_images`: A device's documents fill its image slots from slot 0 in document order and hold 8 images or fewer together; some document holds exactly 8. `plan`: entry s of device d's row is -1 exactly when slot s holds no image, else k * 4 + w with k from 0 to 4 and d + k a device of dp: the image goes to work slot w of device d + k. Each work slot receives at most one image; a device sends at most one image for each k from 1 to 4; some device sends one for every such k and fills its own 4 work slots.
All inputs are finite; a program needn't handle non-finite values.
Results may differ from the reference program's by a relative error of at most 0.0096.
Values may be sent and summed in bfloat16 or wider, within the bound.
A program may use at most 64 MiB of HBM per device.

```python
import jax
import jax.numpy as jnp
from jax import lax

D = 1536
HEADS = 16
HEAD = 64
LATENTS = 64
TOKENS_IMG = 256
WORK = 4
REACH = 4
DOCS_DEV = 2
CAP = 8
INNER = 1024
SOURCES = 1024
SLOTS = 512
N_DP = 128
N_MP = 4


def plan_tables(key):
    device_count = N_DP
    key_surplus, key_own, key_split = jax.random.split(jax.random.fold_in(key, 11), 3)
    raw_surplus = jax.random.randint(key_surplus, (device_count,), 0, 2 * REACH + 1)
    surplus_wish = jnp.maximum(raw_surplus - REACH, 0).astype(jnp.int32)
    own_wish = jax.random.randint(key_own, (device_count,), 0, WORK + 1).astype(jnp.int32)
    steps_back = jnp.arange(1, REACH + 1, dtype=jnp.int32)
    forced = device_count - 1 - REACH

    def advance(recent, inputs):
        index, wish, own = inputs
        incoming = jnp.sum((recent >= steps_back).astype(jnp.int32))
        quiet = (index >= forced - REACH) & (index < forced)
        surplus = jnp.where((incoming > 0) | (index >= device_count - REACH) | quiet, 0, wish)
        surplus = jnp.where(index == forced, REACH, surplus).astype(jnp.int32)
        local = jnp.where(surplus > 0, WORK, jnp.minimum(own, WORK - incoming)).astype(jnp.int32)
        recent = jnp.concatenate([surplus[None], recent[:-1]])
        return (recent, (surplus, local))
    device_iota = jnp.arange(device_count, dtype=jnp.int32)
    unused, (surplus, local) = lax.scan(advance, jnp.zeros((REACH,), jnp.int32), (device_iota, surplus_wish, own_wish))
    padded = jnp.concatenate([jnp.zeros((REACH,), jnp.int32), surplus])
    arrivals = [jnp.zeros((device_count,), jnp.int32)]
    for offset in range(1, REACH + 1):
        earlier = lax.dynamic_slice_in_dim(padded, REACH - offset, device_count)
        arrivals.append((earlier >= offset).astype(jnp.int32))
    arrive_table = jnp.stack(arrivals, 0)
    rank_table = jnp.cumsum(arrive_table, axis=0) - arrive_table
    slot_iota = jnp.arange(CAP, dtype=jnp.int32)
    far_step = (slot_iota[None, :] - WORK + 1) * jnp.ones((device_count, 1), jnp.int32)
    is_far = (far_step >= 1) & (far_step <= surplus[:, None])
    helper_index = jnp.clip(device_iota[:, None] + far_step, 0, device_count - 1)
    step_index = jnp.clip(far_step, 0, REACH)
    far_slot = local[helper_index] + rank_table[step_index, helper_index]
    is_near = slot_iota[None, :] < local[:, None]
    plan_codes = jnp.where(is_near, slot_iota[None, :], jnp.where(is_far, far_step * WORK + far_slot, -1)).astype(jnp.int32)
    loads = local + surplus
    cuts = jax.random.randint(key_split, (device_count, DOCS_DEV - 1), 0, 1 << 20) % (loads[:, None] + 1)
    cuts = jnp.where(device_iota[:, None] == forced, 0, cuts)
    cuts = jnp.sort(cuts, axis=1)
    bounds = jnp.concatenate([jnp.zeros((device_count, 1), jnp.int32), cuts.astype(jnp.int32), loads[:, None]], 1)
    counts = (bounds[:, 1:] - bounds[:, :-1]).astype(jnp.int32)
    return (counts.reshape(-1), plan_codes)


def draw_doc_images(key, part):
    counts, plan_codes = plan_tables(key)
    return counts


def draw_plan(key, part):
    counts, plan_codes = plan_tables(key)
    return plan_codes


def draw_queries(key, part):
    base = jax.random.normal(key, (LATENTS, INNER), jnp.float32)
    return jnp.clip(base, -4.0, 4.0).astype(jnp.bfloat16)


def draw_cotangent(key, part):
    sub = jax.random.fold_in(key, 23)
    base = jax.random.normal(sub, (SLOTS, LATENTS, D), jnp.float32)
    return jnp.clip(base, -6.0, 6.0).astype(jnp.bfloat16)


def raised(drawn, stream_key, source, target, parts, factor):
    owner, partner = [(jnp.arange(drawn.shape[dim]) // (drawn.shape[dim] // parts)).reshape([-1 if axis == dim else 1 for axis in range(drawn.ndim)]) for dim in (source, target)]
    chosen = jax.random.permutation(stream_key, parts)[partner]
    strong = (owner == chosen) | (owner == (partner + parts // 2) % parts)
    return jnp.where(strong, factor * drawn, drawn)


def shard_levels(key, shape, cuts, least, top_value):
    gain = 1.0
    for dim, blocks in cuts:
        heights = jax.random.uniform(jax.random.fold_in(jax.random.fold_in(key, 6), dim), (blocks,), jnp.float32, least / len(cuts), top_value / len(cuts))
        gain = gain * jnp.repeat(jnp.exp(heights), shape[dim] // blocks).reshape((-1,) + (1,) * (len(shape) - 1 - dim))
    return gain


def scatter_about(own_key, extent, deviation, most, pieces=(), held_as=jnp.bfloat16):
    drawn = deviation * jax.random.normal(own_key, extent, jnp.float32)
    if pieces:
        drawn = drawn * shard_levels(own_key, extent, pieces, -0.22, 0.18)
    return jnp.clip(drawn, -most, most).astype(held_as)


def noise_with(stream_key, extent, width, limit, pieces, heavy, kind=jnp.bfloat16):
    values = width * jax.random.normal(stream_key, extent, jnp.float32)
    if pieces:
        values = values * shard_levels(stream_key, extent, pieces, -0.22, 0.18)
    return jnp.clip(raised(values, jax.random.fold_in(stream_key, 3), *heavy), -limit, limit).astype(kind)


def setup_inputs(seed: int = 0) -> dict:
    key_of = jax.random.split(jax.random.key(seed), 11)
    return {
        "media": noise_with(key_of[0], (SOURCES, TOKENS_IMG, D), 1.0, 24.0, ((0, 128), (2, 4)), (0, 2, 128, 5.5)),
        "time_table": scatter_about(key_of[1], (CAP, D), 0.7, 4.0, ((1, 4),)),
        "doc_images": draw_doc_images(jax.random.fold_in(key_of[10], 71), 0),
        "plan": draw_plan(jax.random.fold_in(key_of[10], 71), 0),
        "latents": scatter_about(key_of[4], (LATENTS, D), 1.0, 6.0),
        "queries": draw_queries(jax.random.fold_in(key_of[10], 71), 0),
        "key_weight": scatter_about(key_of[6], (D, INNER), D ** -0.5, 0.15625, ((1, 4),)),
        "value_weight": scatter_about(key_of[7], (D, INNER), D ** -0.5, 0.15625, ((1, 4),)),
        "out_weight": scatter_about(key_of[8], (INNER, D), INNER ** -0.5, 0.1875, ((0, 4),)),
        "cotangent": draw_cotangent(jax.random.fold_in(key_of[10], 71), 0),
    }


norm_epsilon = 1e-05

def layer_norm(rows_in):
    average = lax.optimization_barrier(jnp.mean(rows_in, axis=-1, keepdims=True))
    centred = rows_in - average
    spread = lax.optimization_barrier(jnp.mean(centred * centred, axis=-1, keepdims=True))
    return centred * lax.rsqrt(spread + norm_epsilon)

def reference(media, time_table, doc_images, plan, latents, queries, key_weight, value_weight, out_weight, cotangent):
    slot_iota = jnp.arange(CAP, dtype=jnp.int32)
    counts = doc_images.reshape(N_DP, DOCS_DEV)
    doc_ends = jnp.cumsum(counts, axis=1)
    starts = doc_ends - counts
    start_of = lax.optimization_barrier(jnp.max(jnp.where(starts[:, None, :] <= slot_iota[None, :, None], starts[:, None, :], 0), axis=2))
    position = (slot_iota[None, :] - start_of).astype(jnp.int32)
    time_rows = time_table.astype(jnp.float32)[position]
    framed = (media.astype(jnp.float32).reshape(N_DP, CAP, TOKENS_IMG, D) + time_rows[:, :, None, :]).astype(jnp.bfloat16)
    is_live = plan >= 0
    helper = jnp.where(is_live, plan // WORK, 0)
    target = jnp.where(is_live, plan % WORK, 0)
    device_iota = jnp.arange(N_DP, dtype=jnp.int32)
    destination = jnp.where(is_live, (device_iota[:, None] + helper) * WORK + target, SLOTS).astype(jnp.int32).reshape(-1)
    work_media = jnp.zeros((SLOTS + 1, TOKENS_IMG, D), jnp.bfloat16).at[destination].set(framed.reshape(-1, TOKENS_IMG, D))[:SLOTS]
    alive_slot = jnp.zeros((SLOTS + 1,), jnp.float32).at[destination].set(1.0)[:SLOTS]
    latent_norm = layer_norm(latents.astype(jnp.float32)).astype(jnp.bfloat16)
    latent_keys = jnp.dot(latent_norm, key_weight, preferred_element_type=jnp.float32).astype(jnp.bfloat16)
    latent_values = jnp.dot(latent_norm, value_weight, preferred_element_type=jnp.float32).astype(jnp.bfloat16)
    query_heads = queries.astype(jnp.float32).reshape(LATENTS, HEADS, HEAD)
    group_cols = INNER // N_MP
    out_groups = out_weight.astype(jnp.float32).reshape(N_MP, group_cols, D)
    latents32 = latents.astype(jnp.float32)

    def one_slot(carry, inputs):
        key_acc, value_acc = carry
        image_rows, cot_rows, alive_one = inputs
        normed = layer_norm(image_rows.astype(jnp.float32)).astype(jnp.bfloat16)
        key_rows = jnp.concatenate([jnp.dot(normed, key_weight, preferred_element_type=jnp.float32).astype(jnp.bfloat16), latent_keys], 0)
        value_rows = jnp.concatenate([jnp.dot(normed, value_weight, preferred_element_type=jnp.float32).astype(jnp.bfloat16), latent_values], 0)
        key_heads = key_rows.astype(jnp.float32).reshape(-1, HEADS, HEAD)
        value_heads = value_rows.astype(jnp.float32).reshape(-1, HEADS, HEAD)
        scores = jnp.einsum('qhe,khe->hqk', query_heads, key_heads) * 0.125
        attention = jax.nn.softmax(scores, axis=-1)
        attention_b = attention.astype(jnp.bfloat16)
        attended = jnp.einsum('hqk,khe->qhe', attention_b.astype(jnp.float32), value_heads).reshape(LATENTS, INNER).astype(jnp.bfloat16)
        partial_g = jnp.einsum('qgc,gcd->gqd', attended.astype(jnp.float32).reshape(LATENTS, N_MP, group_cols), out_groups).astype(jnp.bfloat16)
        resampled_one = ((latents32 + lax.optimization_barrier(jnp.sum(partial_g.astype(jnp.float32), axis=0))) * alive_one).astype(jnp.bfloat16)
        cot_live = cot_rows * alive_one.astype(jnp.bfloat16)
        grad_attended = jnp.dot(cot_live, out_weight.T, preferred_element_type=jnp.float32).astype(jnp.bfloat16)
        grad_heads = grad_attended.astype(jnp.float32).reshape(LATENTS, HEADS, HEAD)
        grad_weights = jnp.einsum('qhe,khe->hqk', grad_heads, value_heads)
        row_dot = lax.optimization_barrier(jnp.sum(attention * grad_weights, axis=-1, keepdims=True))
        grad_scores = attention * (grad_weights - row_dot)
        grad_keys = (jnp.einsum('hqk,qhe->khe', grad_scores, query_heads, precision=lax.Precision.HIGHEST) * 0.125).reshape(-1, INNER).astype(jnp.bfloat16)
        grad_values = jnp.einsum('hqk,qhe->khe', attention_b.astype(jnp.float32), grad_heads).reshape(-1, INNER).astype(jnp.bfloat16)
        context = jnp.concatenate([normed, latent_norm], 0)
        key_acc = key_acc + jnp.dot(context.T, grad_keys, preferred_element_type=jnp.float32)
        value_acc = value_acc + jnp.dot(context.T, grad_values, preferred_element_type=jnp.float32)
        return ((key_acc, value_acc), resampled_one)
    start_acc = (jnp.zeros((D, INNER), jnp.float32), jnp.zeros((D, INNER), jnp.float32))
    (key_acc, value_acc), resampled = lax.scan(one_slot, start_acc, (work_media, cotangent, alive_slot))
    return (resampled, key_acc / SLOTS, value_acc / SLOTS)
```

```python
import functools

import jax
import jax.numpy as jnp
from jax import lax
from jax.experimental import pallas as pl
from jax.experimental.pallas import tpu as pltpu
from jax.sharding import PartitionSpec as P

HEAD = 64
MESH = pl.DeviceIdType.MESH
CHUNKS = 4
REACH = 4

norm_epsilon = 1e-05


def plan_scalars(plan_ref, docs_ref, slots, work):
    far_slot = [jnp.int32(0)] * (REACH + 1)
    far_work = [jnp.int32(-1)] * (REACH + 1)
    own_slot = [jnp.int32(0)] * work
    own_live = [jnp.int32(0)] * work
    for s in range(slots):
        code = plan_ref[0, s]
        for k in range(1, REACH + 1):
            inside = (code >= k * work) & (code < (k + 1) * work)
            far_slot[k] = jnp.where(inside, s, far_slot[k])
            far_work[k] = jnp.where(inside, code - k * work, far_work[k])
        for w in range(work):
            own_slot[w] = jnp.where(code == w, s, own_slot[w])
            own_live[w] = jnp.where(code == w, 1, own_live[w])
    first = docs_ref[0]

    def position(s):
        return s - jnp.where(s >= first, first, 0)

    return far_slot, far_work, own_slot, own_live, position


def gather_body(
    n_dp,
    n_mp,
    plan_ref,
    docs_ref,
    media_ref,
    time_ref,
    cot_ref,
    full_ref,
    alive_ref,
    send_buf,
    head_buf,
    got_buf,
    got_head,
    far_send,
    far_recv,
    head_send,
    head_recv,
    ring_send,
    ring_recv,
):
    slots, tokens, quarter = media_ref.shape
    work = cot_ref.shape[0]
    rows = tokens // CHUNKS
    half = work // 2
    me_d = lax.axis_index("dp")
    me_m = lax.axis_index("mp")

    def far(k):
        return lax.rem(me_d + (k + n_dp), n_dp)

    right, left = lax.rem(me_m + 1, n_mp), lax.rem(me_m + n_mp - 1, n_mp)
    opposite = lax.rem(me_m + 2, n_mp)
    barrier = pltpu.get_barrier_semaphore()
    for k in range(1, REACH + 1):
        for to in (far(k), far(-k)):
            pl.semaphore_signal(
                barrier, inc=1, device_id={"dp": to, "mp": me_m}, device_id_type=MESH
            )
    for to in (right, left):
        pl.semaphore_signal(barrier, inc=1, device_id={"dp": me_d, "mp": to}, device_id_type=MESH)

    far_slot, far_work, own_slot, own_live, position = plan_scalars(
        plan_ref, docs_ref, slots, work
    )
    times = time_ref[...].astype(jnp.float32)
    time_rows = lax.broadcasted_iota(jnp.int32, times.shape, 0)

    def time_of(s):
        return jnp.sum(jnp.where(time_rows == position(s), times, 0.0), axis=0, keepdims=True)

    mark_rows = lax.broadcasted_iota(jnp.int32, head_buf.shape[1:], 0)
    for k in range(1, REACH + 1):
        head_buf[k - 1] = jnp.where(mark_rows == far_work[k], 1.0, 0.0).astype(jnp.bfloat16)
        row = time_of(far_slot[k])
        for c in range(CHUNKS):
            send_buf[c, k - 1] = (
                media_ref[far_slot[k], c * rows : (c + 1) * rows, :].astype(jnp.float32) + row
            ).astype(jnp.bfloat16)
    own_rows = [time_of(own_slot[w]) for w in range(work)]

    pl.semaphore_wait(barrier, 2 * REACH + 2)

    def ring_copy(src, dst, i, to):
        return pltpu.make_async_remote_copy(
            src_ref=src,
            dst_ref=dst,
            send_sem=ring_send.at[i],
            recv_sem=ring_recv.at[i],
            device_id={"dp": me_d, "mp": to},
            device_id_type=MESH,
        )

    def own_sends(c, src):
        return [
            ring_copy(src, full_ref.at[me_m, c], 4 * c, right),
            ring_copy(src, full_ref.at[me_m, c], 4 * c + 1, left),
        ]

    def own_arrivals(c):
        return [
            ring_copy(full_ref.at[left, c], full_ref.at[left, c], 4 * c, right),
            ring_copy(full_ref.at[right, c], full_ref.at[right, c], 4 * c + 1, left),
        ]

    def forwards(c):
        first = full_ref.at[left, c, pl.ds(0, half)]
        second = full_ref.at[right, c, pl.ds(half, half)]
        return [
            ring_copy(first, first, 4 * c + 2, right),
            ring_copy(second, second, 4 * c + 3, left),
        ]

    def forward_arrivals(c):
        first = full_ref.at[opposite, c, pl.ds(0, half)]
        second = full_ref.at[opposite, c, pl.ds(half, half)]
        return [
            ring_copy(first, first, 4 * c + 2, right),
            ring_copy(second, second, 4 * c + 3, left),
        ]

    def far_copy(c, k):
        return pltpu.make_async_remote_copy(
            src_ref=send_buf.at[c, k - 1],
            dst_ref=got_buf.at[c, k - 1],
            send_sem=far_send.at[c, k - 1],
            recv_sem=far_recv.at[c, k - 1],
            device_id={"dp": far(k), "mp": me_m},
            device_id_type=MESH,
        )

    def head_copy(k):
        return pltpu.make_async_remote_copy(
            src_ref=head_buf.at[k - 1],
            dst_ref=got_head.at[k - 1],
            send_sem=head_send.at[k - 1],
            recv_sem=head_recv.at[k - 1],
            device_id={"dp": far(k), "mp": me_m},
            device_id_type=MESH,
        )

    started = own_sends(CHUNKS, cot_ref)
    for copy in started:
        copy.start()
    for k in range(REACH, 0, -1):
        head_copy(k).start()
    for c in range(CHUNKS):
        for k in range(REACH, 0, -1):
            far_copy(c, k).start()
    full_ref[me_m, CHUNKS] = cot_ref[...]

    for k in range(1, REACH + 1):
        head_copy(k).wait_recv()
    marks = [got_head[k].astype(jnp.float32) for k in range(REACH)]
    lives = [jnp.where(own_live[w] == 1, 1.0, 0.0) for w in range(work)]
    for w in range(work):
        total = marks[0][w : w + 1, :128]
        for k in range(1, REACH):
            total = total + marks[k][w : w + 1, :128]
        alive_ref[w : w + 1, :] = total + lives[w]

    def place(c):
        for k in range(1, REACH + 1):
            far_copy(c, k).wait_recv()
        for w in range(work):
            block = media_ref[own_slot[w], c * rows : (c + 1) * rows, :].astype(jnp.float32)
            block = (block + own_rows[w]) * lives[w]
            for k in range(REACH):
                block = block + marks[k][w : w + 1, :] * got_buf[c, k].astype(jnp.float32)
            full_ref[me_m, c, w] = block.astype(jnp.bfloat16)
        copies = own_sends(c, full_ref.at[me_m, c])
        for copy in copies:
            copy.start()
        return copies

    order = [CHUNKS] + list(range(CHUNKS))
    for i, c in enumerate(order):
        if i < CHUNKS:
            started += place(i)
        for copy in own_arrivals(c):
            copy.wait_recv()
        for copy in forwards(c):
            copy.start()
            started.append(copy)
    for c in order:
        for copy in forward_arrivals(c):
            copy.wait_recv()
    for copy in started:
        copy.wait_send()
    for k in range(1, REACH + 1):
        head_copy(k).wait_send()
        for c in range(CHUNKS):
            far_copy(c, k).wait_send()


def gather(n_dp, n_mp, plan, docs, media, times, cot):
    slots, tokens, quarter = media.shape
    work, latent_count = cot.shape[:2]
    rows = tokens // CHUNKS
    bf16 = jnp.bfloat16
    vmem = pl.BlockSpec(memory_space=pltpu.VMEM)
    smem = pl.BlockSpec(memory_space=pltpu.SMEM)
    dma = pltpu.SemaphoreType.DMA
    return pl.pallas_call(
        functools.partial(gather_body, n_dp, n_mp),
        name="route_and_gather",
        out_shape=(
            jax.ShapeDtypeStruct((n_mp, CHUNKS + 1, work, rows, quarter), bf16),
            jax.ShapeDtypeStruct((8, 128), jnp.float32),
        ),
        in_specs=[smem, smem, vmem, vmem, vmem],
        out_specs=(vmem, vmem),
        scratch_shapes=[
            pltpu.VMEM((CHUNKS, REACH, rows, quarter), bf16),
            pltpu.VMEM((REACH, 16, quarter), bf16),
            pltpu.VMEM((CHUNKS, REACH, rows, quarter), bf16),
            pltpu.VMEM((REACH, 16, quarter), bf16),
            dma((CHUNKS, REACH)),
            dma((CHUNKS, REACH)),
            dma((REACH,)),
            dma((REACH,)),
            dma((4 * CHUNKS + 4,)),
            dma((4 * CHUNKS + 4,)),
        ],
        compiler_params=pltpu.CompilerParams(
            collective_id=0, has_side_effects=True, vmem_limit_bytes=48 << 20
        ),
    )(plan, docs, media, times, cot)


def in_blocks(x, dim, size):
    shape = x.shape
    pieces = x.reshape(*shape[:dim], size, shape[dim] // size, *shape[dim + 1 :])
    return jnp.moveaxis(pieces, dim, 0)


def summed_on_arrival(x, axis, dim):
    size = lax.axis_size(axis)
    pieces = lax.all_to_all(in_blocks(x, dim, size), axis, 0, 0, tiled=True)
    return jnp.sum(pieces.astype(jnp.float32), axis=0)


def sum_in_two_steps(x, axes, dim):
    far, near = axes
    own = summed_on_arrival(in_blocks(x, dim, lax.axis_size(far)), near, dim + 1)
    return jnp.sum(
        lax.all_to_all(own.astype(jnp.bfloat16), far, 0, 0, tiled=True).astype(jnp.float32), axis=0
    )


def layer_norm(rows_in):
    average = jnp.mean(rows_in, axis=-1, keepdims=True)
    centred = rows_in - average
    spread = jnp.mean(centred * centred, axis=-1, keepdims=True)
    return centred * lax.rsqrt(spread + norm_epsilon)


def local(
    media,
    time_table,
    doc_images,
    plan,
    latents,
    queries,
    key_weight,
    value_weight,
    out_weight,
    cotangent,
):
    image_tokens = media.shape[1]
    quarter = media.shape[2]
    work_slots = cotangent.shape[0]
    latent_count = cotangent.shape[1]
    model_width = latents.shape[1]
    inner_dev = queries.shape[1]
    head_count = inner_dev // HEAD
    context_rows = image_tokens + latent_count
    n_mp = lax.axis_size("mp")
    full, alive = gather(lax.axis_size("dp"), n_mp, plan, doc_images, media, time_table, cotangent)
    alive_slot = alive[:work_slots, 0]
    whole = full.transpose(2, 1, 3, 0, 4).reshape(work_slots, image_tokens + latent_count, model_width)
    full_media, cot_full = whole[:, :image_tokens], whole[:, image_tokens:]
    normed = layer_norm(full_media.astype(jnp.float32)).astype(jnp.bfloat16)
    normed_flat = normed.reshape(work_slots * image_tokens, model_width)
    latent_norm = layer_norm(latents.astype(jnp.float32)).astype(jnp.bfloat16)
    media_keys = (
        jnp.dot(normed_flat, key_weight, preferred_element_type=jnp.float32)
        .astype(jnp.bfloat16)
        .reshape(work_slots, image_tokens, inner_dev)
    )
    media_values = (
        jnp.dot(normed_flat, value_weight, preferred_element_type=jnp.float32)
        .astype(jnp.bfloat16)
        .reshape(work_slots, image_tokens, inner_dev)
    )
    latent_keys = jnp.dot(latent_norm, key_weight, preferred_element_type=jnp.float32).astype(
        jnp.bfloat16
    )
    latent_values = jnp.dot(latent_norm, value_weight, preferred_element_type=jnp.float32).astype(
        jnp.bfloat16
    )
    key_rows = jnp.concatenate(
        [media_keys, jnp.broadcast_to(latent_keys[None], (work_slots, latent_count, inner_dev))], 1
    )
    value_rows = jnp.concatenate(
        [
            media_values,
            jnp.broadcast_to(latent_values[None], (work_slots, latent_count, inner_dev)),
        ],
        1,
    )
    key_heads = key_rows.reshape(work_slots, context_rows, head_count, HEAD)
    value_heads = value_rows.reshape(work_slots, context_rows, head_count, HEAD)
    query_heads = queries.reshape(latent_count, head_count, HEAD)
    scores = (
        jnp.einsum("qhe,wkhe->whqk", query_heads, key_heads, preferred_element_type=jnp.float32)
        * 0.125
    )
    attention = jax.nn.softmax(scores, axis=-1)
    attention_b = attention.astype(jnp.bfloat16)
    attended = jnp.einsum(
        "whqk,wkhe->wqhe", attention_b, value_heads, preferred_element_type=jnp.float32
    ).astype(jnp.bfloat16)
    attended_flat = attended.reshape(work_slots * latent_count, inner_dev)
    partial_out = jnp.dot(attended_flat, out_weight, preferred_element_type=jnp.float32).reshape(
        work_slots, latent_count, model_width
    )
    summed_heads = summed_on_arrival(partial_out.astype(jnp.bfloat16), "mp", 2)
    latent_part = lax.dynamic_slice_in_dim(
        latents, lax.axis_index("mp") * quarter, quarter, 1
    ).astype(jnp.float32)
    resampled = ((latent_part[None] + summed_heads) * alive_slot[:, None, None]).astype(
        jnp.bfloat16
    )
    cot_live = cot_full * alive_slot.astype(jnp.bfloat16)[:, None, None]
    grad_attended = lax.dot_general(
        cot_live.reshape(work_slots * latent_count, model_width),
        out_weight,
        (((1,), (1,)), ((), ())),
        preferred_element_type=jnp.float32,
    ).astype(jnp.bfloat16)
    grad_heads = grad_attended.reshape(work_slots, latent_count, head_count, HEAD)
    grad_weights = jnp.einsum(
        "wqhe,wkhe->whqk", grad_heads, value_heads, preferred_element_type=jnp.float32
    )
    row_dot = jnp.sum(attention * grad_weights, axis=-1, keepdims=True)
    grad_scores = attention * (grad_weights - row_dot)
    grad_keys = (
        (
            jnp.einsum(
                "whqk,qhe->wkhe",
                grad_scores,
                query_heads.astype(jnp.float32),
                precision=lax.Precision.HIGHEST,
            )
            * 0.125
        )
        .astype(jnp.bfloat16)
        .reshape(work_slots, context_rows, inner_dev)
    )
    grad_values = (
        jnp.einsum("whqk,wqhe->wkhe", attention_b, grad_heads, preferred_element_type=jnp.float32)
        .astype(jnp.bfloat16)
        .reshape(work_slots, context_rows, inner_dev)
    )
    media_grads = jnp.concatenate(
        [grad_keys[:, :image_tokens], grad_values[:, :image_tokens]], 2
    ).reshape(work_slots * image_tokens, 2 * inner_dev)
    latent_grads = jnp.concatenate(
        [
            jnp.sum(grad_keys[:, image_tokens:].astype(jnp.float32), axis=0),
            jnp.sum(grad_values[:, image_tokens:].astype(jnp.float32), axis=0),
        ],
        1,
    )
    latent_norm32 = latent_norm.astype(jnp.float32)
    inverse_slots = 1.0 / (lax.axis_size("dp") * work_slots)
    media_part = lax.dot_general(
        normed_flat, media_grads, (((0,), (0,)), ((), ())), preferred_element_type=jnp.float32
    )
    latent_term = lax.dot_general(
        latent_norm32,
        latent_grads,
        (((0,), (0,)), ((), ())),
        precision=lax.Precision.HIGHEST,
        preferred_element_type=jnp.float32,
    )
    shares = summed_on_arrival(((media_part + latent_term) * inverse_slots).astype(jnp.bfloat16), "dp", 0)
    return (resampled, shares[:, :inner_dev], shares[:, inner_dev:])


def solution(mesh):
    return jax.shard_map(
        local,
        mesh=mesh,
        in_specs=(
            P("dp", None, "mp"),
            P(None, "mp"),
            P("dp"),
            P("dp", None),
            P(),
            P(None, "mp"),
            P(None, "mp"),
            P(None, "mp"),
            P("mp", None),
            P("dp", None, "mp"),
        ),
        out_specs=(P("dp", None, "mp"), P("dp", "mp"), P("dp", "mp")),
        check_vma=False,
    )
```

```python
import functools

import jax
import jax.numpy as jnp
from jax import lax
from jax.experimental import pallas as pl
from jax.experimental.pallas import tpu as pltpu
from jax.sharding import PartitionSpec as P

HEAD = 64
MESH = pl.DeviceIdType.MESH
CHUNKS = 4
REACH = 4

norm_epsilon = 1e-05


def plan_scalars(plan_ref, docs_ref, slots, work):
    far_slot = [jnp.int32(0)] * (REACH + 1)
    far_work = [jnp.int32(-1)] * (REACH + 1)
    own_slot = [jnp.int32(0)] * work
    own_live = [jnp.int32(0)] * work
    for s in range(slots):
        code = plan_ref[0, s]
        for k in range(1, REACH + 1):
            inside = (code >= k * work) & (code < (k + 1) * work)
            far_slot[k] = jnp.where(inside, s, far_slot[k])
            far_work[k] = jnp.where(inside, code - k * work, far_work[k])
        for w in range(work):
            own_slot[w] = jnp.where(code == w, s, own_slot[w])
            own_live[w] = jnp.where(code == w, 1, own_live[w])
    first = docs_ref[0]

    def position(s):
        return s - jnp.where(s >= first, first, 0)

    return far_slot, far_work, own_slot, own_live, position


def gather_body(
    n_dp,
    n_mp,
    plan_ref,
    docs_ref,
    media_ref,
    time_ref,
    cot_ref,
    full_ref,
    alive_ref,
    send_buf,
    head_buf,
    got_buf,
    got_head,
    far_send,
    far_recv,
    head_send,
    head_recv,
    ring_send,
    ring_recv,
):
    slots, tokens, quarter = media_ref.shape
    work = cot_ref.shape[0]
    rows = tokens // CHUNKS
    half = work // 2
    me_d = lax.axis_index("dp")
    me_m = lax.axis_index("mp")

    def far(k):
        return lax.rem(me_d + (k + n_dp), n_dp)

    right, left = lax.rem(me_m + 1, n_mp), lax.rem(me_m + n_mp - 1, n_mp)
    opposite = lax.rem(me_m + 2, n_mp)
    barrier = pltpu.get_barrier_semaphore()
    for k in range(1, REACH + 1):
        for to in (far(k), far(-k)):
            pl.semaphore_signal(
                barrier, inc=1, device_id={"dp": to, "mp": me_m}, device_id_type=MESH
            )
    for to in (right, left):
        pl.semaphore_signal(barrier, inc=1, device_id={"dp": me_d, "mp": to}, device_id_type=MESH)

    far_slot, far_work, own_slot, own_live, position = plan_scalars(
        plan_ref, docs_ref, slots, work
    )
    times = time_ref[...].astype(jnp.float32)
    time_rows = lax.broadcasted_iota(jnp.int32, times.shape, 0)

    def time_of(s):
        return jnp.sum(jnp.where(time_rows == position(s), times, 0.0), axis=0, keepdims=True)

    mark_rows = lax.broadcasted_iota(jnp.int32, head_buf.shape[1:], 0)
    for k in range(1, REACH + 1):
        head_buf[k - 1] = jnp.where(mark_rows == far_work[k], 1.0, 0.0).astype(jnp.bfloat16)
        row = time_of(far_slot[k])
        for c in range(CHUNKS):
            send_buf[c, k - 1] = (
                media_ref[far_slot[k], c * rows : (c + 1) * rows, :].astype(jnp.float32) + row
            ).astype(jnp.bfloat16)
    own_rows = [time_of(own_slot[w]) for w in range(work)]

    pl.semaphore_wait(barrier, 2 * REACH + 2)

    def ring_copy(src, dst, i, to):
        return pltpu.make_async_remote_copy(
            src_ref=src,
            dst_ref=dst,
            send_sem=ring_send.at[i],
            recv_sem=ring_recv.at[i],
            device_id={"dp": me_d, "mp": to},
            device_id_type=MESH,
        )

    def own_sends(c, src):
        return [
            ring_copy(src, full_ref.at[me_m, c], 4 * c, right),
            ring_copy(src, full_ref.at[me_m, c], 4 * c + 1, left),
        ]

    def own_arrivals(c):
        return [
            ring_copy(full_ref.at[left, c], full_ref.at[left, c], 4 * c, right),
            ring_copy(full_ref.at[right, c], full_ref.at[right, c], 4 * c + 1, left),
        ]

    def forwards(c):
        first = full_ref.at[left, c, pl.ds(0, half)]
        second = full_ref.at[right, c, pl.ds(half, half)]
        return [
            ring_copy(first, first, 4 * c + 2, right),
            ring_copy(second, second, 4 * c + 3, left),
        ]

    def forward_arrivals(c):
        first = full_ref.at[opposite, c, pl.ds(0, half)]
        second = full_ref.at[opposite, c, pl.ds(half, half)]
        return [
            ring_copy(first, first, 4 * c + 2, right),
            ring_copy(second, second, 4 * c + 3, left),
        ]

    def far_copy(c, k):
        return pltpu.make_async_remote_copy(
            src_ref=send_buf.at[c, k - 1],
            dst_ref=got_buf.at[c, k - 1],
            send_sem=far_send.at[c, k - 1],
            recv_sem=far_recv.at[c, k - 1],
            device_id={"dp": far(k), "mp": me_m},
            device_id_type=MESH,
        )

    def head_copy(k):
        return pltpu.make_async_remote_copy(
            src_ref=head_buf.at[k - 1],
            dst_ref=got_head.at[k - 1],
            send_sem=head_send.at[k - 1],
            recv_sem=head_recv.at[k - 1],
            device_id={"dp": far(k), "mp": me_m},
            device_id_type=MESH,
        )

    started = own_sends(CHUNKS, cot_ref)
    for copy in started:
        copy.start()
    for k in range(REACH, 0, -1):
        head_copy(k).start()
    for c in range(CHUNKS):
        for k in range(REACH, 0, -1):
            far_copy(c, k).start()
    full_ref[me_m, CHUNKS] = cot_ref[...]

    for k in range(1, REACH + 1):
        head_copy(k).wait_recv()
    marks = [got_head[k].astype(jnp.float32) for k in range(REACH)]
    lives = [jnp.where(own_live[w] == 1, 1.0, 0.0) for w in range(work)]
    for w in range(work):
        total = marks[0][w : w + 1, :128]
        for k in range(1, REACH):
            total = total + marks[k][w : w + 1, :128]
        alive_ref[w : w + 1, :] = total + lives[w]

    def place(c):
        for k in range(1, REACH + 1):
            far_copy(c, k).wait_recv()
        for w in range(work):
            block = media_ref[own_slot[w], c * rows : (c + 1) * rows, :].astype(jnp.float32)
            block = (block + own_rows[w]) * lives[w]
            for k in range(REACH):
                block = block + marks[k][w : w + 1, :] * got_buf[c, k].astype(jnp.float32)
            full_ref[me_m, c, w] = block.astype(jnp.bfloat16)
        copies = own_sends(c, full_ref.at[me_m, c])
        for copy in copies:
            copy.start()
        return copies

    order = [CHUNKS] + list(range(CHUNKS))
    for i, c in enumerate(order):
        if i < CHUNKS:
            started += place(i)
        for copy in own_arrivals(c):
            copy.wait_recv()
        for copy in forwards(c):
            copy.start()
            started.append(copy)
    for c in order:
        for copy in forward_arrivals(c):
            copy.wait_recv()
    for copy in started:
        copy.wait_send()
    for k in range(1, REACH + 1):
        head_copy(k).wait_send()
        for c in range(CHUNKS):
            far_copy(c, k).wait_send()


def gather(n_dp, n_mp, plan, docs, media, times, cot):
    slots, tokens, quarter = media.shape
    work, latent_count = cot.shape[:2]
    rows = tokens // CHUNKS
    bf16 = jnp.bfloat16
    vmem = pl.BlockSpec(memory_space=pltpu.VMEM)
    smem = pl.BlockSpec(memory_space=pltpu.SMEM)
    dma = pltpu.SemaphoreType.DMA
    return pl.pallas_call(
        functools.partial(gather_body, n_dp, n_mp),
        name="route_and_gather",
        out_shape=(
            jax.ShapeDtypeStruct((n_mp, CHUNKS + 1, work, rows, quarter), bf16),
            jax.ShapeDtypeStruct((8, 128), jnp.float32),
        ),
        in_specs=[smem, smem, vmem, vmem, vmem],
        out_specs=(vmem, vmem),
        scratch_shapes=[
            pltpu.VMEM((CHUNKS, REACH, rows, quarter), bf16),
            pltpu.VMEM((REACH, 16, quarter), bf16),
            pltpu.VMEM((CHUNKS, REACH, rows, quarter), bf16),
            pltpu.VMEM((REACH, 16, quarter), bf16),
            dma((CHUNKS, REACH)),
            dma((CHUNKS, REACH)),
            dma((REACH,)),
            dma((REACH,)),
            dma((4 * CHUNKS + 4,)),
            dma((4 * CHUNKS + 4,)),
        ],
        compiler_params=pltpu.CompilerParams(
            collective_id=0, has_side_effects=True, vmem_limit_bytes=48 << 20
        ),
    )(plan, docs, media, times, cot)


def attend_body(
    full_ref,
    alive_ref,
    latents_ref,
    queries_ref,
    key_weight_ref,
    value_weight_ref,
    out_weight_ref,
    partial_ref,
    grads_ref,
    context,
    cot_live,
    keys,
    values,
    grads,
):
    n_mp, chunks, work, rows, quarter = full_ref.shape
    chunks = chunks - 1
    tokens = chunks * rows
    latent_count, width = latents_ref.shape
    inner = queries_ref.shape[1]
    heads = inner // HEAD
    f32, bf16 = jnp.float32, jnp.bfloat16
    contract_last = (((1,), (1,)), ((), ()))
    contract_first = (((0,), (0,)), ((), ()))

    def dot(a, b, dims=(((1,), (0,)), ((), ()))):
        return lax.dot_general(a, b, dims, preferred_element_type=f32)

    def normalise(parts):
        parts = [p.astype(f32) for p in parts]
        average = sum(jnp.sum(p, axis=-1, keepdims=True) for p in parts) * (1.0 / width)
        parts = [p - average for p in parts]
        spread = sum(jnp.sum(p * p, axis=-1, keepdims=True) for p in parts) * (1.0 / width)
        scale = lax.rsqrt(spread + norm_epsilon)
        return [(p * scale).astype(bf16) for p in parts]

    latent_norm = normalise([latents_ref[...]])[0]
    for w in range(work):
        context[work * tokens + w * latent_count : work * tokens + (w + 1) * latent_count, :] = (
            latent_norm
        )
    latent_keys = dot(latent_norm, key_weight_ref[...]).astype(bf16)
    latent_values = dot(latent_norm, value_weight_ref[...]).astype(bf16)

    def project(i, carry):
        c, w = i // work, i % work
        at = pl.multiple_of(w * tokens + c * rows, rows)
        pieces = normalise([full_ref[m, c, w] for m in range(n_mp)])
        for m in range(n_mp):
            context[pl.ds(at, rows), m * quarter : (m + 1) * quarter] = pieces[m]
        return carry

    lax.fori_loop(0, chunks * work, project, 0)

    def project_slot(w, carry):
        at = pl.multiple_of(w * tokens, tokens)
        normed = context[pl.ds(at, tokens), :]
        keys[pl.ds(at, tokens), :] = dot(normed, key_weight_ref[...]).astype(bf16)
        values[pl.ds(at, tokens), :] = dot(normed, value_weight_ref[...]).astype(bf16)
        return carry

    lax.fori_loop(0, work, project_slot, 0)

    row_head = lax.broadcasted_iota(jnp.int32, (heads * latent_count, inner), 0) // latent_count
    col_head = lax.broadcasted_iota(jnp.int32, (heads * latent_count, inner), 1) // HEAD
    same_head = row_head == col_head

    def spread_heads(x):
        return jnp.where(same_head, jnp.concatenate([x.astype(f32)] * heads, axis=0), 0.0)

    wide_queries32 = spread_heads(queries_ref[...])
    wide_queries = wide_queries32.astype(bf16)
    wide_queries_t = wide_queries32.T.astype(bf16)
    latent_scores = dot(latent_keys, wide_queries, contract_last) * 0.125

    for w in range(work):
        alive = jnp.concatenate([alive_ref[w : w + 1, :]] * (quarter // 128), axis=1)
        for m in range(n_mp):
            cot_live[w * latent_count : (w + 1) * latent_count, m * quarter : (m + 1) * quarter] = (
                full_ref[m, chunks, w].astype(f32) * alive
            ).astype(bf16)
    grad_attended = dot(cot_live[...], out_weight_ref[...], contract_last)

    for w in range(work):
        at = w * tokens
        slot_keys = keys[at : at + tokens, :]
        slot_values = values[at : at + tokens, :]
        scores = dot(slot_keys, wide_queries, contract_last) * 0.125
        top = jnp.maximum(
            jnp.max(scores, axis=0, keepdims=True), jnp.max(latent_scores, axis=0, keepdims=True)
        )
        weight = jnp.exp(scores - top)
        latent_weight = jnp.exp(latent_scores - top)
        total = jnp.sum(weight, axis=0, keepdims=True) + jnp.sum(
            latent_weight, axis=0, keepdims=True
        )
        attention = weight / total
        latent_attention = latent_weight / total
        attention_b = attention.astype(bf16)
        latent_attention_b = latent_attention.astype(bf16)
        attended = dot(attention_b, slot_values, contract_first) + dot(
            latent_attention_b, latent_values, contract_first
        )
        attended = jnp.where(same_head, attended, 0.0)
        attended = sum(
            attended[h * latent_count : (h + 1) * latent_count, :] for h in range(heads)
        ).astype(bf16)
        partial = dot(attended, out_weight_ref[...]).astype(bf16)
        for m in range(n_mp):
            partial_ref[m, w] = partial[:, m * quarter : (m + 1) * quarter]

        slot_grad = grad_attended[w * latent_count : (w + 1) * latent_count, :].astype(bf16)
        wide_grad32 = spread_heads(slot_grad)
        wide_grad = wide_grad32.astype(bf16)
        wide_grad_t = wide_grad32.T.astype(bf16)
        slope = dot(slot_values, wide_grad, contract_last)
        latent_slope = dot(latent_values, wide_grad, contract_last)
        row_dot = jnp.sum(attention * slope, axis=0, keepdims=True) + jnp.sum(
            latent_attention * latent_slope, axis=0, keepdims=True
        )
        for where, count, att, att_b, slopes in (
            (at, tokens, attention, attention_b, slope),
            (work * tokens + w * latent_count, latent_count, latent_attention, latent_attention_b, latent_slope),
        ):
            grad_scores = att * (slopes - row_dot)
            high = grad_scores.astype(bf16)
            low = (grad_scores - high.astype(f32)).astype(bf16)
            grad_keys = (
                dot(wide_queries_t, high, contract_last) + dot(wide_queries_t, low, contract_last)
            ) * 0.125
            grads[0:inner, where : where + count] = grad_keys.astype(bf16)
            grads[inner : 2 * inner, where : where + count] = dot(
                wide_grad_t, att_b, contract_last
            ).astype(bf16)

    inverse = 1.0 / (n_mp_dp_slots(work))
    for kind in range(2):
        for m in range(n_mp):
            grads_ref[kind, m] = (
                dot(
                    grads[kind * inner : (kind + 1) * inner, :],
                    context[:, m * quarter : (m + 1) * quarter],
                )
                * inverse
            ).astype(bf16)


def n_mp_dp_slots(work):
    return lax.axis_size("dp") * work


def attend(full, alive, latents, queries, key_weight, value_weight, out_weight):
    n_mp, parts, work, rows, quarter = full.shape
    tokens = (parts - 1) * rows
    latent_count, width = latents.shape
    inner = queries.shape[1]
    context_rows = work * (tokens + latent_count)
    bf16 = jnp.bfloat16
    vmem = pl.BlockSpec(memory_space=pltpu.VMEM)
    return pl.pallas_call(
        attend_body,
        name="attend",
        out_shape=(
            jax.ShapeDtypeStruct((n_mp, work, latent_count, quarter), bf16),
            jax.ShapeDtypeStruct((2, n_mp, inner, quarter), bf16),
        ),
        in_specs=[vmem] * 7,
        out_specs=(vmem, vmem),
        scratch_shapes=[
            pltpu.VMEM((context_rows, width), bf16),
            pltpu.VMEM((work * latent_count, width), bf16),
            pltpu.VMEM((work * tokens, inner), bf16),
            pltpu.VMEM((work * tokens, inner), bf16),
            pltpu.VMEM((2 * inner, context_rows), bf16),
        ],
        compiler_params=pltpu.CompilerParams(vmem_limit_bytes=56 << 20),
    )(full, alive, latents, queries, key_weight, value_weight, out_weight)


DEPTH = 16
CORES = 2


def reduce_body(
    n_dp,
    n_mp,
    partial_ref,
    grads_ref,
    alive_ref,
    latents_ref,
    resampled_ref,
    key_ref,
    value_ref,
    y_relay,
    y_sum,
    y_got,
    core_got,
    x_sum,
    x_relay,
    x_got,
    z_send,
    z_got,
    last,
    last_got,
    y_sems,
    core_sems,
    x_sems,
    z_sems,
    last_sems,
):
    f32, bf16 = jnp.float32, jnp.bfloat16
    work, latent_count, quarter = resampled_ref.shape
    inner = key_ref.shape[1]
    n_x = n_dp // (DEPTH * CORES)
    me_d = lax.axis_index("dp")
    me_m = lax.axis_index("mp")
    me_core = lax.rem(me_d, CORES)
    me_z = lax.rem(me_d // CORES, DEPTH)
    me_x = me_d // (DEPTH * CORES)

    def at(x, z, core):
        return (x * DEPTH + z) * CORES + core

    y_right, y_left = lax.rem(me_m + 1, n_mp), lax.rem(me_m + n_mp - 1, n_mp)
    y_far = lax.rem(me_m + 2, n_mp)
    x_right, x_left = lax.rem(me_x + 1, n_x), lax.rem(me_x + n_x - 1, n_x)
    x_far = lax.rem(me_x + 2, n_x)
    other = 1 - me_core
    dp_right, dp_left = at(x_right, me_z, me_core), at(x_left, me_z, me_core)
    dp_other = at(me_x, me_z, other)

    def z_of(o):
        return lax.rem(me_z + o, DEPTH)

    barrier = pltpu.get_barrier_semaphore()
    partners = [(me_d, y_right), (me_d, y_left)]
    partners += [(d, me_m) for d in (dp_right, dp_left, dp_other)]
    partners += [(at(me_x, z_of(o), me_core), me_m) for o in range(1, DEPTH)]
    for d, m in partners:
        pl.semaphore_signal(barrier, inc=1, device_id={"dp": d, "mp": m}, device_id_type=MESH)
    pl.semaphore_wait(barrier, len(partners))

    def remote(src, dst, sems, i, d, m):
        return pltpu.make_async_remote_copy(
            src_ref=src,
            dst_ref=dst,
            send_sem=sems.at[0, i],
            recv_sem=sems.at[1, i],
            device_id={"dp": d, "mp": m},
            device_id_type=MESH,
        )

    half_w = work // 2
    low, high = pl.ds(0, half_w), pl.ds(half_w, half_w)
    half_r = inner // 2
    top, bottom = pl.ds(0, half_r), pl.ds(half_r, half_r)
    y_copies = [
        remote(partial_ref.at[y_far, low], y_relay.at[0], y_sems, 0, me_d, y_right),
        remote(partial_ref.at[y_far, high], y_relay.at[1], y_sems, 1, me_d, y_left),
        remote(partial_ref.at[y_right, high], y_got.at[0, high], y_sems, 2, me_d, y_right),
        remote(partial_ref.at[y_left, low], y_got.at[1, low], y_sems, 3, me_d, y_left),
        remote(y_sum.at[0], y_got.at[0, low], y_sems, 4, me_d, y_right),
        remote(y_sum.at[1], y_got.at[1, high], y_sems, 5, me_d, y_left),
    ]
    x_copies = [
        remote(x_sum.at[x_far, top], x_relay.at[0], x_sems, 0, dp_right, me_m),
        remote(x_sum.at[x_far, bottom], x_relay.at[1], x_sems, 1, dp_left, me_m),
        remote(x_sum.at[x_right, bottom], x_got.at[0, bottom], x_sems, 2, dp_right, me_m),
        remote(x_sum.at[x_left, top], x_got.at[1, top], x_sems, 3, dp_left, me_m),
        remote(x_sum.at[x_right, top], x_got.at[0, top], x_sems, 4, dp_right, me_m),
        remote(x_sum.at[x_left, bottom], x_got.at[1, bottom], x_sems, 5, dp_left, me_m),
    ]
    order = (x_far, x_right, x_left, me_x)
    other_order = order
    core_copies = [
        remote(grads_ref.at[other, x], core_got.at[x], core_sems, i, dp_other, me_m)
        for i, x in enumerate(other_order)
    ]
    for i in range(4):
        core_copies[i].start()
        y_copies[i].start()

    def join_cores(i):
        core_copies[i].wait_recv()
        x = order[i]
        x_sum[x] = (grads_ref[me_core, x].astype(f32) + core_got[x].astype(f32)).astype(bf16)

    join_cores(0)
    x_copies[0].start()
    x_copies[1].start()
    join_cores(1)
    x_copies[2].start()
    join_cores(2)
    x_copies[3].start()

    y_copies[0].wait_recv()
    y_sum[0] = (partial_ref[y_right, low].astype(f32) + y_relay[0].astype(f32)).astype(bf16)
    y_copies[4].start()
    y_copies[1].wait_recv()
    y_sum[1] = (partial_ref[y_left, high].astype(f32) + y_relay[1].astype(f32)).astype(bf16)
    y_copies[5].start()

    join_cores(3)
    x_copies[0].wait_recv()
    x_sum[x_right, top] = (x_sum[x_right, top].astype(f32) + x_relay[0].astype(f32)).astype(bf16)
    x_copies[4].start()
    x_copies[1].wait_recv()
    x_sum[x_left, bottom] = (x_sum[x_left, bottom].astype(f32) + x_relay[1].astype(f32)).astype(
        bf16
    )
    x_copies[5].start()
    for i in range(2, 6):
        x_copies[i].wait_recv()
    total = x_sum[me_x].astype(f32) + x_got[0].astype(f32) + x_got[1].astype(f32)
    rows = total.T
    share = quarter // DEPTH
    for z in range(DEPTH):
        piece = rows[z * share : (z + 1) * share, :]
        z_send[z] = jnp.concatenate([piece[:, :128], piece[:, 128:]], axis=0).astype(bf16)
    z_copies = {
        o: remote(
            z_send.at[z_of(o)],
            z_got.at[o - 1],
            z_sems,
            o - 1,
            at(me_x, z_of(o), me_core),
            me_m,
        )
        for o in range(1, DEPTH)
    }
    for o in sorted(range(1, DEPTH), key=lambda o: -min(o, DEPTH - o)):
        z_copies[o].start()

    for i in range(2, 6):
        y_copies[i].wait_recv()
    mine = latents_ref[:, pl.ds(pl.multiple_of(me_m * quarter, 128), quarter)].astype(f32)
    for w in range(work):
        alive = jnp.concatenate([alive_ref[w : w + 1, :]] * (quarter // 128), axis=1)
        summed = partial_ref[me_m, w].astype(f32) + y_got[0, w].astype(f32)
        summed = summed + y_got[1, w].astype(f32)
        resampled_ref[w] = ((mine + summed) * alive).astype(bf16)

    total = z_send[me_z].astype(f32)
    for o in sorted(range(1, DEPTH), key=lambda o: min(o, DEPTH - o)):
        z_copies[o].wait_recv()
        total = total + z_got[o - 1].astype(f32)
    last[...] = total
    last_copy = remote(last, last_got, last_sems, 0, dp_other, me_m)
    last_copy.start()
    last_copy.wait_recv()
    first_core = me_core == 0
    ours, theirs = last[...], last_got[...]
    for out, block in (
        (key_ref, jnp.where(first_core, ours, theirs)),
        (value_ref, jnp.where(first_core, theirs, ours)),
    ):
        each = share // CORES
        for half in range(2):
            piece = block[half * share : (half + 1) * share, :]
            out[:, half * 128 : (half + 1) * 128] = jnp.where(
                first_core, piece[:each, :], piece[each:, :]
            )
    for copy in y_copies + x_copies + core_copies + list(z_copies.values()) + [last_copy]:
        copy.wait_send()


def reduce(n_dp, n_mp, partial, grads, alive, latents):
    work, latent_count, quarter = partial.shape[1:]
    inner = grads.shape[2]
    n_x = n_dp // (DEPTH * CORES)
    f32, bf16 = jnp.float32, jnp.bfloat16
    vmem = pl.BlockSpec(memory_space=pltpu.VMEM)
    dma = pltpu.SemaphoreType.DMA
    share = quarter // DEPTH
    half = (2, work // 2, latent_count, quarter)
    return pl.pallas_call(
        functools.partial(reduce_body, n_dp, n_mp),
        name="reduce",
        out_shape=(
            jax.ShapeDtypeStruct((work, latent_count, quarter), bf16),
            jax.ShapeDtypeStruct((share // CORES, inner), f32),
            jax.ShapeDtypeStruct((share // CORES, inner), f32),
        ),
        in_specs=[vmem] * 4,
        out_specs=(vmem,) * 3,
        scratch_shapes=[
            pltpu.VMEM(half, bf16),
            pltpu.VMEM(half, bf16),
            pltpu.VMEM((2, work, latent_count, quarter), bf16),
            pltpu.VMEM((n_x, inner, quarter), bf16),
            pltpu.VMEM((n_x, inner, quarter), bf16),
            pltpu.VMEM((2, inner // 2, quarter), bf16),
            pltpu.VMEM((2, inner, quarter), bf16),
            pltpu.VMEM((DEPTH, 2 * share, 128), bf16),
            pltpu.VMEM((DEPTH - 1, 2 * share, 128), bf16),
            pltpu.VMEM((2 * share, 128), f32),
            pltpu.VMEM((2 * share, 128), f32),
            dma((2, 6)),
            dma((2, n_x)),
            dma((2, 6)),
            dma((2, DEPTH - 1)),
            dma((2, 1)),
        ],
        compiler_params=pltpu.CompilerParams(
            collective_id=1, has_side_effects=True, vmem_limit_bytes=48 << 20
        ),
    )(partial, grads, alive, latents)


def local(
    media,
    time_table,
    doc_images,
    plan,
    latents,
    queries,
    key_weight,
    value_weight,
    out_weight,
    cotangent,
):
    n_dp, n_mp = lax.axis_size("dp"), lax.axis_size("mp")
    full, alive = gather(n_dp, n_mp, plan, doc_images, media, time_table, cotangent)
    partial_out, grads = attend(
        full, alive, latents, queries, key_weight, value_weight, out_weight
    )
    return reduce(n_dp, n_mp, partial_out, grads, alive, latents)


def solution(mesh):
    return jax.shard_map(
        local,
        mesh=mesh,
        in_specs=(
            P("dp", None, "mp"),
            P(None, "mp"),
            P("dp"),
            P("dp", None),
            P(),
            P(None, "mp"),
            P(None, "mp"),
            P(None, "mp"),
            P("mp", None),
            P("dp", None, "mp"),
        ),
        out_specs=(P("dp", None, "mp"), P("dp", "mp"), P("dp", "mp")),
        check_vma=False,
    )
```

```python
import functools

import jax
import jax.numpy as jnp
from jax import lax
from jax.experimental import pallas as pl
from jax.experimental.pallas import tpu as pltpu
from jax.sharding import PartitionSpec as P

HEAD = 64
MESH = pl.DeviceIdType.MESH
CHUNKS = 4
REACH = 4

DEPTH = 16
CORES = 2

norm_epsilon = 1e-05


def plan_scalars(plan_ref, docs_ref, slots, work):
    far_slot = [jnp.int32(0)] * (REACH + 1)
    far_work = [jnp.int32(-1)] * (REACH + 1)
    own_slot = [jnp.int32(0)] * work
    own_live = [jnp.int32(0)] * work
    for s in range(slots):
        code = plan_ref[0, s]
        for k in range(1, REACH + 1):
            inside = (code >= k * work) & (code < (k + 1) * work)
            far_slot[k] = jnp.where(inside, s, far_slot[k])
            far_work[k] = jnp.where(inside, code - k * work, far_work[k])
        for w in range(work):
            own_slot[w] = jnp.where(code == w, s, own_slot[w])
            own_live[w] = jnp.where(code == w, 1, own_live[w])
    first = docs_ref[0]

    def position(s):
        return s - jnp.where(s >= first, first, 0)

    return far_slot, far_work, own_slot, own_live, position


def normalise(parts, width):
    parts = [p.astype(jnp.float32) for p in parts]
    average = sum(jnp.sum(p, axis=-1, keepdims=True) for p in parts) * (1.0 / width)
    parts = [p - average for p in parts]
    spread = sum(jnp.sum(p * p, axis=-1, keepdims=True) for p in parts) * (1.0 / width)
    scale = lax.rsqrt(spread + norm_epsilon)
    return [(p * scale).astype(jnp.bfloat16) for p in parts]


def dot(a, b, dims=(1, 0)):
    return lax.dot_general(
        a, b, (((dims[0],), (dims[1],)), ((), ())), preferred_element_type=jnp.float32
    )


def body(
    n_dp,
    n_mp,
    plan_hbm,
    docs_hbm,
    time_hbm,
    media_hbm,
    cot_hbm,
    queries_hbm,
    latents_hbm,
    key_weight_hbm,
    value_weight_hbm,
    out_weight_hbm,
    resampled_ref,
    key_ref,
    value_ref,
    plan_ref,
    docs_ref,
    time_ref,
    media_ref,
    queries_ref,
    latents_ref,
    key_weight_ref,
    value_weight_ref,
    out_weight_ref,
    send_buf,
    head_buf,
    got_buf,
    got_head,
    full,
    context,
    cot_live,
    keys,
    values,
    grad_attended,
    grads,
    partial,
    y_relay,
    y_sum,
    y_got,
    core_send,
    core_got,
    x_own,
    x_sum,
    x_relay,
    x_got,
    z_send,
    z_got,
    last,
    last_got,
    local_sems,
    far_sems,
    head_sems,
    ring_sems,
    y_sems,
    core_sems,
    x_sems,
    z_sems,
    last_sems,
):
    f32, bf16 = jnp.float32, jnp.bfloat16
    slots, tokens, quarter = media_hbm.shape
    work, latent_count = cot_hbm.shape[:2]
    width = latents_hbm.shape[1]
    inner = queries_hbm.shape[1]
    heads = inner // HEAD
    rows = tokens // CHUNKS
    half_w = work // 2
    n_x = n_dp // (DEPTH * CORES)
    me_d = lax.axis_index("dp")
    me_m = lax.axis_index("mp")
    me_core = lax.rem(me_d, CORES)
    me_z = lax.rem(me_d // CORES, DEPTH)
    me_x = me_d // (DEPTH * CORES)

    def at(x, z, core):
        return (x * DEPTH + z) * CORES + core

    def far(k):
        return lax.rem(me_d + (k + n_dp), n_dp)

    def z_of(o):
        return lax.rem(me_z + o, DEPTH)

    y_right, y_left = lax.rem(me_m + 1, n_mp), lax.rem(me_m + n_mp - 1, n_mp)
    y_far = lax.rem(me_m + 2, n_mp)
    x_right, x_left = lax.rem(me_x + 1, n_x), lax.rem(me_x + n_x - 1, n_x)
    x_far = lax.rem(me_x + 2, n_x)
    other = 1 - me_core
    dp_right, dp_left = at(x_right, me_z, me_core), at(x_left, me_z, me_core)
    dp_other = at(me_x, me_z, other)

    arguments = [
        (plan_hbm, plan_ref),
        (docs_hbm, docs_ref),
        (time_hbm, time_ref),
    ]
    arguments += [
        (media_hbm, media_ref),
        (cot_hbm, full.at[me_m, CHUNKS]),
        (latents_hbm, latents_ref),
        (key_weight_hbm, key_weight_ref),
        (value_weight_hbm, value_weight_ref),
        (queries_hbm, queries_ref),
        (out_weight_hbm, out_weight_ref),
    ]
    loads = [
        pltpu.make_async_copy(src, dst, local_sems.at[i]) for i, (src, dst) in enumerate(arguments)
    ]
    for load in loads:
        load.start()

    barrier = pltpu.get_barrier_semaphore()
    partners = [(at(me_x, z_of(o), me_core), me_m) for o in range(DEPTH - 1, 0, -1)]
    for k in range(1, REACH + 1):
        partners += [(far(k), me_m), (far(-k), me_m)]
    partners += [(d, me_m) for d in (dp_right, dp_left, dp_other)]
    partners += [(me_d, y_right), (me_d, y_left)]
    for d, m in partners:
        pl.semaphore_signal(barrier, inc=1, device_id={"dp": d, "mp": m}, device_id_type=MESH)

    for load in loads[:4]:
        load.wait()
    far_slot, far_work, own_slot, own_live, position = plan_scalars(
        plan_ref, docs_ref, slots, work
    )
    times = time_ref[...].astype(f32)
    time_rows = lax.broadcasted_iota(jnp.int32, times.shape, 0)

    def time_of(s):
        return jnp.sum(jnp.where(time_rows == position(s), times, 0.0), axis=0, keepdims=True)

    mark_rows = lax.broadcasted_iota(jnp.int32, head_buf.shape[1:], 0)
    far_rows = [None]
    for k in range(1, REACH + 1):
        head_buf[k - 1] = jnp.where(mark_rows == far_work[k], 1.0, 0.0).astype(bf16)
        far_rows.append(time_of(far_slot[k]))
    own_rows = [time_of(own_slot[w]) for w in range(work)]
    for c in range(CHUNKS):
        for k in range(1, REACH + 1):
            block = media_ref[far_slot[k], c * rows : (c + 1) * rows, :].astype(f32)
            send_buf[c, k - 1] = (block + far_rows[k]).astype(bf16)

    pl.semaphore_wait(barrier, len(partners))

    def remote(src, dst, sems, i, d, m):
        return pltpu.make_async_remote_copy(
            src_ref=src,
            dst_ref=dst,
            send_sem=sems.at[0, i],
            recv_sem=sems.at[1, i],
            device_id={"dp": d, "mp": m},
            device_id_type=MESH,
        )

    def own_sends(c, src):
        return [
            remote(src, full.at[me_m, c], ring_sems, 4 * c, me_d, y_right),
            remote(src, full.at[me_m, c], ring_sems, 4 * c + 1, me_d, y_left),
        ]

    def own_arrivals(c):
        return [
            remote(full.at[y_left, c], full.at[y_left, c], ring_sems, 4 * c, me_d, y_right),
            remote(full.at[y_right, c], full.at[y_right, c], ring_sems, 4 * c + 1, me_d, y_left),
        ]

    low, high = pl.ds(0, half_w), pl.ds(half_w, half_w)

    def forwards(c):
        first, second = full.at[y_left, c, low], full.at[y_right, c, high]
        return [
            remote(first, first, ring_sems, 4 * c + 2, me_d, y_right),
            remote(second, second, ring_sems, 4 * c + 3, me_d, y_left),
        ]

    def forward_arrivals(c):
        first, second = full.at[y_far, c, low], full.at[y_far, c, high]
        return [
            remote(first, first, ring_sems, 4 * c + 2, me_d, y_right),
            remote(second, second, ring_sems, 4 * c + 3, me_d, y_left),
        ]

    def far_copy(c, k):
        i = c * REACH + k - 1
        return remote(send_buf.at[c, k - 1], got_buf.at[c, k - 1], far_sems, i, far(k), me_m)

    def head_copy(k):
        return remote(head_buf.at[k - 1], got_head.at[k - 1], head_sems, k - 1, far(k), me_m)

    started = own_sends(CHUNKS, cot_hbm)
    for k in range(REACH, 0, -1):
        started.append(head_copy(k))
    for c in range(CHUNKS):
        for k in range(REACH, 0, -1):
            started.append(far_copy(c, k))
    for copy in started:
        copy.start()

    first_weight = 5
    for load in loads[first_weight - 1 : first_weight + 4]:
        load.wait()
    latent_norm = normalise([latents_ref[...]], width)[0]
    for w in range(work):
        where = work * tokens + w * latent_count
        context[where : where + latent_count, :] = latent_norm
    latent_keys = dot(latent_norm, key_weight_ref[...]).astype(bf16)
    latent_values = dot(latent_norm, value_weight_ref[...]).astype(bf16)
    row_head = lax.broadcasted_iota(jnp.int32, (heads * latent_count, inner), 0) // latent_count
    col_head = lax.broadcasted_iota(jnp.int32, (heads * latent_count, inner), 1) // HEAD
    same_head = row_head == col_head

    def spread_heads(x):
        return jnp.where(same_head, jnp.concatenate([x.astype(f32)] * heads, axis=0), 0.0)

    wide_queries32 = spread_heads(queries_ref[...])
    wide_queries = wide_queries32.astype(bf16)
    wide_queries_t = wide_queries32.T.astype(bf16)
    latent_scores = dot(latent_keys, wide_queries, (1, 1)) * 0.125
    loads[first_weight + 4].wait()

    for k in range(1, REACH + 1):
        head_copy(k).wait_recv()
    marks = [got_head[k].astype(f32) for k in range(REACH)]
    lives = [jnp.where(own_live[w] == 1, 1.0, 0.0) for w in range(work)]
    alive = [sum(marks[k][w : w + 1, :] for k in range(REACH)) + lives[w] for w in range(work)]

    def place(c):
        for k in range(1, REACH + 1):
            far_copy(c, k).wait_recv()
        for w in range(work):
            block = media_ref[own_slot[w], c * rows : (c + 1) * rows, :].astype(f32)
            block = (block + own_rows[w]) * lives[w]
            for k in range(REACH):
                block = block + marks[k][w : w + 1, :] * got_buf[c, k].astype(f32)
            full[me_m, c, w] = block.astype(bf16)
        return own_sends(c, full.at[me_m, c])

    sub = min(32, rows)

    def project(c):
        def norm_rows(i, carry):
            w, r = i // (rows // sub), i % (rows // sub)
            r = pl.multiple_of(r * sub, sub)
            pieces = normalise([full[m, c, w, pl.ds(r, sub), :] for m in range(n_mp)], width)
            where = pl.multiple_of(w * tokens + c * rows + r, sub)
            for m in range(n_mp):
                context[pl.ds(where, sub), m * quarter : (m + 1) * quarter] = pieces[m]
            return carry

        lax.fori_loop(0, work * (rows // sub), norm_rows, 0)
        places = [slice(w * tokens + c * rows, w * tokens + (c + 1) * rows) for w in range(work)]
        normed = jnp.concatenate([context[p, :] for p in places], axis=0)
        for out, weight in ((keys, key_weight_ref), (values, value_weight_ref)):
            product = dot(normed, weight[...]).astype(bf16)
            for w, p in enumerate(places):
                out[p, :] = product[w * rows : (w + 1) * rows, :]

    def pull_back():
        for w in range(work):
            for m in range(n_mp):
                cot_live[
                    w * latent_count : (w + 1) * latent_count, m * quarter : (m + 1) * quarter
                ] = (full[m, CHUNKS, w].astype(f32) * alive[w]).astype(bf16)
        grad_attended[...] = dot(cot_live[...], out_weight_ref[...], (1, 1)).astype(bf16)

    def finish(c):
        for copy in forward_arrivals(c):
            copy.wait_recv()
        if c == CHUNKS:
            pull_back()
        else:
            project(c)

    order = [CHUNKS] + list(range(CHUNKS))
    for i, c in enumerate(order):
        if i < CHUNKS:
            copies = place(i)
            for copy in copies:
                copy.start()
            started += copies
        for copy in own_arrivals(c):
            copy.wait_recv()
        copies = forwards(c)
        for copy in copies:
            copy.start()
        started += copies
        if i > 0:
            finish(order[i - 1])
    finish(order[-1])

    half_r = inner // 2
    top, bottom = pl.ds(0, half_r), pl.ds(half_r, half_r)
    y_copies = [
        remote(partial.at[y_far, low], y_relay.at[0], y_sems, 0, me_d, y_right),
        remote(partial.at[y_far, high], y_relay.at[1], y_sems, 1, me_d, y_left),
        remote(partial.at[y_right, high], y_got.at[0, high], y_sems, 2, me_d, y_right),
        remote(partial.at[y_left, low], y_got.at[1, low], y_sems, 3, me_d, y_left),
        remote(y_sum.at[0], y_got.at[0, low], y_sems, 4, me_d, y_right),
        remote(y_sum.at[1], y_got.at[1, high], y_sems, 5, me_d, y_left),
    ]
    for w in range(work):
        begin = w * tokens
        slot_keys = keys[begin : begin + tokens, :]
        slot_values = values[begin : begin + tokens, :]
        scores = dot(slot_keys, wide_queries, (1, 1)) * 0.125
        top_score = jnp.maximum(
            jnp.max(scores, axis=0, keepdims=True), jnp.max(latent_scores, axis=0, keepdims=True)
        )
        weight = jnp.exp(scores - top_score)
        latent_weight = jnp.exp(latent_scores - top_score)
        total = jnp.sum(weight, axis=0, keepdims=True) + jnp.sum(
            latent_weight, axis=0, keepdims=True
        )
        attention = weight / total
        latent_attention = latent_weight / total
        attention_b = attention.astype(bf16)
        latent_attention_b = latent_attention.astype(bf16)
        attended = dot(attention_b, slot_values, (0, 0)) + dot(
            latent_attention_b, latent_values, (0, 0)
        )
        attended = jnp.where(same_head, attended, 0.0)
        attended = sum(
            attended[h * latent_count : (h + 1) * latent_count, :] for h in range(heads)
        ).astype(bf16)
        part = dot(attended, out_weight_ref[...]).astype(bf16)
        for m in range(n_mp):
            partial[m, w] = part[:, m * quarter : (m + 1) * quarter]
        if w == half_w - 1:
            y_copies[0].start()
            y_copies[3].start()
        if w == work - 1:
            y_copies[1].start()
            y_copies[2].start()

        slot_grad = grad_attended[w * latent_count : (w + 1) * latent_count, :]
        wide_grad32 = spread_heads(slot_grad)
        wide_grad = wide_grad32.astype(bf16)
        wide_grad_t = wide_grad32.T.astype(bf16)
        slope = dot(slot_values, wide_grad, (1, 1))
        latent_slope = dot(latent_values, wide_grad, (1, 1))
        row_dot = jnp.sum(attention * slope, axis=0, keepdims=True) + jnp.sum(
            latent_attention * latent_slope, axis=0, keepdims=True
        )
        for where, count, att, att_b, slopes in (
            (begin, tokens, attention, attention_b, slope),
            (
                work * tokens + w * latent_count,
                latent_count,
                latent_attention,
                latent_attention_b,
                latent_slope,
            ),
        ):
            grad_scores = att * (slopes - row_dot)
            near = grad_scores.astype(bf16)
            rest = (grad_scores - near.astype(f32)).astype(bf16)
            grad_keys = (
                dot(wide_queries_t, near, (1, 1)) + dot(wide_queries_t, rest, (1, 1))
            ) * 0.125
            grads[0:inner, where : where + count] = grad_keys.astype(bf16)
            grads[inner : 2 * inner, where : where + count] = dot(
                wide_grad_t, att_b, (1, 1)
            ).astype(bf16)

    x_copies = [
        remote(x_sum.at[x_far, top], x_relay.at[0], x_sems, 0, dp_right, me_m),
        remote(x_sum.at[x_far, bottom], x_relay.at[1], x_sems, 1, dp_left, me_m),
        remote(x_sum.at[x_right, bottom], x_got.at[0, bottom], x_sems, 2, dp_right, me_m),
        remote(x_sum.at[x_left, top], x_got.at[1, top], x_sems, 3, dp_left, me_m),
        remote(x_sum.at[x_right, top], x_got.at[0, top], x_sems, 4, dp_right, me_m),
        remote(x_sum.at[x_left, bottom], x_got.at[1, bottom], x_sems, 5, dp_left, me_m),
    ]
    x_order = (x_far, x_right, x_left, me_x)
    core_copies = [
        remote(core_send.at[i], core_got.at[i], core_sems, i, dp_other, me_m) for i in range(n_x)
    ]
    inverse = 1.0 / (n_dp * work)

    def weight_grad(kind, x):
        left_side = grads[pl.ds(pl.multiple_of(kind * inner, inner), inner), :]
        right_side = context[:, pl.ds(pl.multiple_of(x * quarter, 128), quarter)]
        return dot(left_side, right_side) * inverse

    def join_cores(i):
        core_copies[i].wait_recv()
        x_sum[x_order[i]] = (x_own[i] + core_got[i].astype(f32)).astype(bf16)
        if i == 0:
            x_copies[0].start()
            x_copies[1].start()
        elif i < 3:
            x_copies[i + 1].start()

    for i, x in enumerate(x_order):
        core_send[i] = weight_grad(other, x).astype(bf16)
        core_copies[i].start()
        x_own[i] = weight_grad(me_core, x)
        if i > 0:
            join_cores(i - 1)

    y_copies[0].wait_recv()
    y_sum[0] = (partial[y_right, low].astype(f32) + y_relay[0].astype(f32)).astype(bf16)
    y_copies[4].start()
    y_copies[1].wait_recv()
    y_sum[1] = (partial[y_left, high].astype(f32) + y_relay[1].astype(f32)).astype(bf16)
    y_copies[5].start()
    join_cores(n_x - 1)
    x_copies[0].wait_recv()
    x_sum[x_right, top] = (x_sum[x_right, top].astype(f32) + x_relay[0].astype(f32)).astype(bf16)
    x_copies[4].start()
    x_copies[1].wait_recv()
    x_sum[x_left, bottom] = (x_sum[x_left, bottom].astype(f32) + x_relay[1].astype(f32)).astype(
        bf16
    )
    x_copies[5].start()
    for i in range(2, 6):
        x_copies[i].wait_recv()
    summed = (x_sum[me_x].astype(f32) + x_got[0].astype(f32) + x_got[1].astype(f32)).T
    share = quarter // DEPTH
    for z in range(DEPTH):
        piece = summed[z * share : (z + 1) * share, :]
        z_send[z] = jnp.concatenate([piece[:, :128], piece[:, 128:]], axis=0).astype(bf16)
    z_copies = {
        o: remote(
            z_send.at[z_of(o)],
            z_got.at[o - 1],
            z_sems,
            o - 1,
            at(me_x, z_of(o), me_core),
            me_m,
        )
        for o in range(1, DEPTH)
    }
    for o in sorted(range(1, DEPTH), key=lambda o: -min(o, DEPTH - o)):
        z_copies[o].start()

    for i in range(2, 6):
        y_copies[i].wait_recv()
    mine = latents_ref[:, pl.ds(pl.multiple_of(me_m * quarter, 128), quarter)].astype(f32)
    for w in range(work):
        heads_sum = partial[me_m, w].astype(f32) + y_got[0, w].astype(f32)
        heads_sum = heads_sum + y_got[1, w].astype(f32)
        resampled_ref[w] = ((mine + heads_sum) * alive[w]).astype(bf16)

    total = z_send[me_z].astype(f32)
    for o in sorted(range(1, DEPTH), key=lambda o: min(o, DEPTH - o)):
        z_copies[o].wait_recv()
        total = total + z_got[o - 1].astype(f32)
    last[...] = total
    last_copy = remote(last, last_got, last_sems, 0, dp_other, me_m)
    last_copy.start()
    last_copy.wait_recv()
    first_core = me_core == 0
    ours, theirs = last[...], last_got[...]
    each = share // CORES
    for out, block in (
        (key_ref, jnp.where(first_core, ours, theirs)),
        (value_ref, jnp.where(first_core, theirs, ours)),
    ):
        for half in range(2):
            piece = block[half * share : (half + 1) * share, :]
            out[:, half * 128 : (half + 1) * 128] = jnp.where(
                first_core, piece[:each, :], piece[each:, :]
            )
    for copy in started + y_copies + x_copies + core_copies + list(z_copies.values()) + [last_copy]:
        copy.wait_send()


def local(
    media,
    time_table,
    doc_images,
    plan,
    latents,
    queries,
    key_weight,
    value_weight,
    out_weight,
    cotangent,
):
    n_dp, n_mp = lax.axis_size("dp"), lax.axis_size("mp")
    slots, tokens, quarter = media.shape
    work, latent_count = cotangent.shape[:2]
    width = latents.shape[1]
    inner = queries.shape[1]
    rows = tokens // CHUNKS
    n_x = n_dp // (DEPTH * CORES)
    share = quarter // DEPTH
    context_rows = work * (tokens + latent_count)
    half = (2, work // 2, latent_count, quarter)
    f32, bf16 = jnp.float32, jnp.bfloat16
    vmem = pl.BlockSpec(memory_space=pltpu.VMEM)
    hbm = pl.BlockSpec(memory_space=pl.ANY)
    dma = pltpu.SemaphoreType.DMA

    def like(x):
        return pltpu.VMEM(x.shape, x.dtype)

    return pl.pallas_call(
        functools.partial(body, n_dp, n_mp),
        name="resample",
        out_shape=(
            jax.ShapeDtypeStruct((work, latent_count, quarter), bf16),
            jax.ShapeDtypeStruct((share // CORES, inner), f32),
            jax.ShapeDtypeStruct((share // CORES, inner), f32),
        ),
        in_specs=[hbm] * 10,
        out_specs=(vmem,) * 3,
        scratch_shapes=[
            pltpu.SMEM(plan.shape, jnp.int32),
            pltpu.SMEM(doc_images.shape, jnp.int32),
            like(time_table),
            like(media),
            like(queries),
            like(latents),
            like(key_weight),
            like(value_weight),
            like(out_weight),
            pltpu.VMEM((CHUNKS, REACH, rows, quarter), bf16),
            pltpu.VMEM((REACH, 16, quarter), bf16),
            pltpu.VMEM((CHUNKS, REACH, rows, quarter), bf16),
            pltpu.VMEM((REACH, 16, quarter), bf16),
            pltpu.VMEM((n_mp, CHUNKS + 1, work, rows, quarter), bf16),
            pltpu.VMEM((context_rows, width), bf16),
            pltpu.VMEM((work * latent_count, width), bf16),
            pltpu.VMEM((work * tokens, inner), bf16),
            pltpu.VMEM((work * tokens, inner), bf16),
            pltpu.VMEM((work * latent_count, inner), bf16),
            pltpu.VMEM((2 * inner, context_rows), bf16),
            pltpu.VMEM((n_mp, work, latent_count, quarter), bf16),
            pltpu.VMEM(half, bf16),
            pltpu.VMEM(half, bf16),
            pltpu.VMEM((2, work, latent_count, quarter), bf16),
            pltpu.VMEM((n_x, inner, quarter), bf16),
            pltpu.VMEM((n_x, inner, quarter), bf16),
            pltpu.VMEM((n_x, inner, quarter), f32),
            pltpu.VMEM((n_x, inner, quarter), bf16),
            pltpu.VMEM((2, inner // 2, quarter), bf16),
            pltpu.VMEM((2, inner, quarter), bf16),
            pltpu.VMEM((DEPTH, 2 * share, 128), bf16),
            pltpu.VMEM((DEPTH - 1, 2 * share, 128), bf16),
            pltpu.VMEM((2 * share, 128), f32),
            pltpu.VMEM((2 * share, 128), f32),
            dma((10,)),
            dma((2, CHUNKS * REACH)),
            dma((2, REACH)),
            dma((2, 4 * CHUNKS + 4)),
            dma((2, 6)),
            dma((2, n_x)),
            dma((2, 6)),
            dma((2, DEPTH - 1)),
            dma((2, 1)),
        ],
        compiler_params=pltpu.CompilerParams(
            collective_id=0, has_side_effects=True, vmem_limit_bytes=60 << 20
        ),
    )(
        plan,
        doc_images,
        time_table,
        media,
        cotangent,
        queries,
        latents,
        key_weight,
        value_weight,
        out_weight,
    )


def solution(mesh):
    return jax.shard_map(
        local,
        mesh=mesh,
        in_specs=(
            P("dp", None, "mp"),
            P(None, "mp"),
            P("dp"),
            P("dp", None),
            P(),
            P(None, "mp"),
            P(None, "mp"),
            P(None, "mp"),
            P("mp", None),
            P("dp", None, "mp"),
        ),
        out_specs=(P("dp", None, "mp"), P("dp", "mp"), P("dp", "mp")),
        check_vma=False,
    )
```

```python
import functools

import jax
import jax.numpy as jnp
from jax import lax
from jax.experimental import pallas as pl
from jax.experimental.pallas import tpu as pltpu
from jax.sharding import PartitionSpec as P

HEAD = 64
MESH = pl.DeviceIdType.MESH
CHUNKS = 4
REACH = 4

DEPTH = 16
CORES = 2

norm_epsilon = 1e-05


def plan_scalars(plan_ref, docs_ref, slots, work):
    far_slot = [jnp.int32(0)] * (REACH + 1)
    far_work = [jnp.int32(-1)] * (REACH + 1)
    own_slot = [jnp.int32(0)] * work
    own_live = [jnp.int32(0)] * work
    for s in range(slots):
        code = plan_ref[0, s]
        for k in range(1, REACH + 1):
            inside = (code >= k * work) & (code < (k + 1) * work)
            far_slot[k] = jnp.where(inside, s, far_slot[k])
            far_work[k] = jnp.where(inside, code - k * work, far_work[k])
        for w in range(work):
            own_slot[w] = jnp.where(code == w, s, own_slot[w])
            own_live[w] = jnp.where(code == w, 1, own_live[w])
    first = docs_ref[0]

    def position(s):
        return s - jnp.where(s >= first, first, 0)

    return far_slot, far_work, own_slot, own_live, position


def normalise(parts, width):
    parts = [p.astype(jnp.float32) for p in parts]
    average = sum(jnp.sum(p, axis=-1, keepdims=True) for p in parts) * (1.0 / width)
    parts = [p - average for p in parts]
    spread = sum(jnp.sum(p * p, axis=-1, keepdims=True) for p in parts) * (1.0 / width)
    scale = lax.rsqrt(spread + norm_epsilon)
    return [(p * scale).astype(jnp.bfloat16) for p in parts]


def dot(a, b, dims=(1, 0)):
    return lax.dot_general(
        a, b, (((dims[0],), (dims[1],)), ((), ())), preferred_element_type=jnp.float32
    )


def body(
    n_dp,
    n_mp,
    plan_hbm,
    docs_hbm,
    time_hbm,
    media_hbm,
    cot_hbm,
    queries_hbm,
    latents_hbm,
    key_weight_hbm,
    value_weight_hbm,
    out_weight_hbm,
    resampled_ref,
    key_ref,
    value_ref,
    plan_ref,
    docs_ref,
    time_ref,
    media_ref,
    queries_ref,
    latents_ref,
    key_weight_ref,
    value_weight_ref,
    out_weight_ref,
    send_buf,
    head_buf,
    got_buf,
    got_head,
    full,
    context,
    cot_live,
    values,
    scores,
    slopes,
    latent_slopes,
    wide_grads,
    wide_grads_t,
    attention,
    grads,
    partial,
    y_relay,
    y_sum,
    y_got,
    core_both,
    core_got,
    x_sum,
    x_relay,
    x_got,
    z_send,
    z_got,
    last,
    last_got,
    local_sems,
    far_sems,
    head_sems,
    ring_sems,
    y_sems,
    core_sems,
    x_sems,
    z_sems,
    last_sems,
    known_sems,
):
    f32, bf16 = jnp.float32, jnp.bfloat16
    slots, tokens, quarter = media_hbm.shape
    work, latent_count = cot_hbm.shape[:2]
    width = latents_hbm.shape[1]
    inner = queries_hbm.shape[1]
    heads = inner // HEAD
    rows = tokens // CHUNKS
    half_w = work // 2
    n_x = n_dp // (DEPTH * CORES)
    me_d = lax.axis_index("dp")
    me_m = lax.axis_index("mp")
    me_core = lax.rem(me_d, CORES)
    me_z = lax.rem(me_d // CORES, DEPTH)
    me_x = me_d // (DEPTH * CORES)

    def at(x, z, core):
        return (x * DEPTH + z) * CORES + core

    def far(k):
        return lax.rem(me_d + (k + n_dp), n_dp)

    def z_of(o):
        return lax.rem(me_z + o, DEPTH)

    y_right, y_left = lax.rem(me_m + 1, n_mp), lax.rem(me_m + n_mp - 1, n_mp)
    y_far = lax.rem(me_m + 2, n_mp)
    x_right, x_left = lax.rem(me_x + 1, n_x), lax.rem(me_x + n_x - 1, n_x)
    x_far = lax.rem(me_x + 2, n_x)
    other = 1 - me_core
    dp_right, dp_left = at(x_right, me_z, me_core), at(x_left, me_z, me_core)
    dp_other = at(me_x, me_z, other)

    arguments = [
        (plan_hbm, plan_ref),
        (docs_hbm, docs_ref),
        (time_hbm, time_ref),
    ]
    arguments += [
        (media_hbm, media_ref),
        (cot_hbm, full.at[me_m, CHUNKS]),
        (latents_hbm, latents_ref),
        (key_weight_hbm, key_weight_ref),
        (value_weight_hbm, value_weight_ref),
        (queries_hbm, queries_ref),
        (out_weight_hbm, out_weight_ref),
    ]
    loads = [
        pltpu.make_async_copy(src, dst, local_sems.at[i]) for i, (src, dst) in enumerate(arguments)
    ]
    for load in loads:
        load.start()

    barrier = pltpu.get_barrier_semaphore()
    partners = [(at(me_x, z_of(o), me_core), me_m) for o in (2, DEPTH - 2, 1, DEPTH - 1)]
    for k in range(1, REACH + 1):
        partners += [(far(k), me_m), (far(-k), me_m)]
    partners += [(d, me_m) for d in (dp_right, dp_left, dp_other)]
    partners += [(me_d, y_right), (me_d, y_left)]
    for d, m in partners:
        pl.semaphore_signal(barrier, inc=1, device_id={"dp": d, "mp": m}, device_id_type=MESH)

    for load in loads[:4]:
        load.wait()
    far_slot, far_work, own_slot, own_live, position = plan_scalars(
        plan_ref, docs_ref, slots, work
    )
    times = time_ref[...].astype(f32)
    time_rows = lax.broadcasted_iota(jnp.int32, times.shape, 0)

    def time_of(s):
        return jnp.sum(jnp.where(time_rows == position(s), times, 0.0), axis=0, keepdims=True)

    mark_rows = lax.broadcasted_iota(jnp.int32, head_buf.shape[1:], 0)
    far_rows = [None]
    for k in range(1, REACH + 1):
        head_buf[k - 1] = jnp.where(mark_rows == far_work[k], 1.0, 0.0).astype(bf16)
        far_rows.append(time_of(far_slot[k]))
    own_rows = [time_of(own_slot[w]) for w in range(work)]
    for c in range(CHUNKS):
        for k in range(1, REACH + 1):
            block = media_ref[far_slot[k], c * rows : (c + 1) * rows, :].astype(f32)
            send_buf[c, k - 1] = (block + far_rows[k]).astype(bf16)

    pl.semaphore_wait(barrier, len(partners))

    def greet(i, distance):
        for o in (distance, DEPTH - distance):
            pl.semaphore_signal(
                known_sems.at[i],
                inc=1,
                device_id={"dp": at(me_x, z_of(o), me_core), "mp": me_m},
                device_id_type=MESH,
            )

    greet(0, 2)

    def remote(src, dst, sems, i, d, m):
        return pltpu.make_async_remote_copy(
            src_ref=src,
            dst_ref=dst,
            send_sem=sems.at[0, i],
            recv_sem=sems.at[1, i],
            device_id={"dp": d, "mp": m},
            device_id_type=MESH,
        )

    def own_sends(c, src):
        return [
            remote(src, full.at[me_m, c], ring_sems, 4 * c, me_d, y_right),
            remote(src, full.at[me_m, c], ring_sems, 4 * c + 1, me_d, y_left),
        ]

    def own_arrivals(c):
        return [
            remote(full.at[y_left, c], full.at[y_left, c], ring_sems, 4 * c, me_d, y_right),
            remote(full.at[y_right, c], full.at[y_right, c], ring_sems, 4 * c + 1, me_d, y_left),
        ]

    low, high = pl.ds(0, half_w), pl.ds(half_w, half_w)

    def forwards(c):
        first, second = full.at[y_left, c, low], full.at[y_right, c, high]
        return [
            remote(first, first, ring_sems, 4 * c + 2, me_d, y_right),
            remote(second, second, ring_sems, 4 * c + 3, me_d, y_left),
        ]

    def forward_arrivals(c):
        first, second = full.at[y_far, c, low], full.at[y_far, c, high]
        return [
            remote(first, first, ring_sems, 4 * c + 2, me_d, y_right),
            remote(second, second, ring_sems, 4 * c + 3, me_d, y_left),
        ]

    def far_copy(c, k):
        i = c * REACH + k - 1
        return remote(send_buf.at[c, k - 1], got_buf.at[c, k - 1], far_sems, i, far(k), me_m)

    def head_copy(k):
        return remote(head_buf.at[k - 1], got_head.at[k - 1], head_sems, k - 1, far(k), me_m)

    started = own_sends(CHUNKS, cot_hbm)
    for k in range(REACH, 0, -1):
        started.append(head_copy(k))
    for c in range(CHUNKS):
        for k in range(REACH, 0, -1):
            started.append(far_copy(c, k))
    for copy in started:
        copy.start()

    first_weight = 5
    for load in loads[first_weight - 1 : first_weight + 4]:
        load.wait()
    latent_norm = normalise([latents_ref[...]], width)[0]
    for w in range(work):
        where = work * tokens + w * latent_count
        for m in range(n_mp):
            context[m, where : where + latent_count, :] = latent_norm[
                :, m * quarter : (m + 1) * quarter
            ]
    latent_keys = dot(latent_norm, key_weight_ref[...]).astype(bf16)
    latent_values = dot(latent_norm, value_weight_ref[...]).astype(bf16)
    row_head = lax.broadcasted_iota(jnp.int32, (heads * latent_count, inner), 0) // latent_count
    col_head = lax.broadcasted_iota(jnp.int32, (heads * latent_count, inner), 1) // HEAD
    same_head = row_head == col_head

    def spread_heads(x):
        return jnp.where(same_head, jnp.concatenate([x.astype(f32)] * heads, axis=0), 0.0)

    wide_queries32 = spread_heads(queries_ref[...])
    wide_queries = wide_queries32.astype(bf16)
    wide_queries_t = wide_queries32.T.astype(bf16)
    latent_scores = dot(latent_keys, wide_queries, (1, 1)) * 0.125
    loads[first_weight + 4].wait()

    for k in range(1, REACH + 1):
        head_copy(k).wait_recv()
    marks = [got_head[k].astype(f32) for k in range(REACH)]
    lives = [jnp.where(own_live[w] == 1, 1.0, 0.0) for w in range(work)]
    alive = [sum(marks[k][w : w + 1, :] for k in range(REACH)) + lives[w] for w in range(work)]

    def place(c):
        for k in range(1, REACH + 1):
            far_copy(c, k).wait_recv()
        for w in range(work):
            block = media_ref[own_slot[w], c * rows : (c + 1) * rows, :].astype(f32)
            block = (block + own_rows[w]) * lives[w]
            for k in range(REACH):
                block = block + marks[k][w : w + 1, :] * got_buf[c, k].astype(f32)
            full[me_m, c, w] = block.astype(bf16)
        return own_sends(c, full.at[me_m, c])

    sub = min(32, rows)

    def project(c):
        def norm_rows(i, carry):
            w, r = i // (rows // sub), i % (rows // sub)
            r = pl.multiple_of(r * sub, sub)
            pieces = normalise([full[m, c, w, pl.ds(r, sub), :] for m in range(n_mp)], width)
            where = pl.multiple_of(w * tokens + c * rows + r, sub)
            for m in range(n_mp):
                context[m, pl.ds(where, sub), :] = pieces[m]
            return carry

        lax.fori_loop(0, work * (rows // sub), norm_rows, 0)
        places = [slice(w * tokens + c * rows, w * tokens + (c + 1) * rows) for w in range(work)]
        normed = [
            jnp.concatenate([context[m, p, :] for p in places], axis=0) for m in range(n_mp)
        ]

        def product(weight):
            return sum(
                dot(normed[m], weight[m * quarter : (m + 1) * quarter, :]) for m in range(n_mp)
            ).astype(bf16)

        new_keys, new_values = product(key_weight_ref), product(value_weight_ref)
        new_scores = dot(new_keys, wide_queries, (1, 1)) * 0.125
        for w, p in enumerate(places):
            values[p, :] = new_values[w * rows : (w + 1) * rows, :]
            scores[p, :] = new_scores[w * rows : (w + 1) * rows, :]
            slopes[p, :] = dot(new_values[w * rows : (w + 1) * rows, :], wide_grads[w], (1, 1))

    def pull_back():
        for w in range(work):
            for m in range(n_mp):
                cot_live[
                    w * latent_count : (w + 1) * latent_count, m * quarter : (m + 1) * quarter
                ] = (full[m, CHUNKS, w].astype(f32) * alive[w]).astype(bf16)
        grad_attended = dot(cot_live[...], out_weight_ref[...], (1, 1)).astype(bf16)
        for w in range(work):
            wide = spread_heads(grad_attended[w * latent_count : (w + 1) * latent_count, :])
            wide_grads[w] = wide.astype(bf16)
            wide_grads_t[w] = wide.T.astype(bf16)
            latent_slopes[w] = dot(latent_values, wide.astype(bf16), (1, 1))

    def finish(c):
        for copy in forward_arrivals(c):
            copy.wait_recv()
        if c == CHUNKS:
            pull_back()
        else:
            project(c)

    pl.semaphore_wait(known_sems.at[0], 2)
    greet(1, 4)
    order = [CHUNKS] + list(range(CHUNKS))
    for i, c in enumerate(order):
        if i < CHUNKS:
            copies = place(i)
            for copy in copies:
                copy.start()
            started += copies
        for copy in own_arrivals(c):
            copy.wait_recv()
        copies = forwards(c)
        for copy in copies:
            copy.start()
        started += copies
        if i > 0:
            finish(order[i - 1])
    finish(order[-1])

    half_r = inner // CORES
    top, bottom = pl.ds(0, half_r // 2), pl.ds(half_r // 2, half_r // 2)
    y_copies = [
        remote(partial.at[y_far, low], y_relay.at[0], y_sems, 0, me_d, y_right),
        remote(partial.at[y_far, high], y_relay.at[1], y_sems, 1, me_d, y_left),
        remote(partial.at[y_right, high], y_got.at[0, high], y_sems, 2, me_d, y_right),
        remote(partial.at[y_left, low], y_got.at[1, low], y_sems, 3, me_d, y_left),
        remote(y_sum.at[0], y_got.at[0, low], y_sems, 4, me_d, y_right),
        remote(y_sum.at[1], y_got.at[1, high], y_sems, 5, me_d, y_left),
    ]
    pl.semaphore_wait(known_sems.at[1], 2)
    extent = tokens + latent_count
    parts = []
    for w in range(work):
        begin = w * tokens
        slot_scores = scores[begin : begin + tokens, :]
        top_score = jnp.maximum(
            jnp.max(slot_scores, axis=0, keepdims=True),
            jnp.max(latent_scores, axis=0, keepdims=True),
        )
        weight = jnp.exp(slot_scores - top_score)
        latent_weight = jnp.exp(latent_scores - top_score)
        total = jnp.sum(weight, axis=0, keepdims=True) + jnp.sum(
            latent_weight, axis=0, keepdims=True
        )
        inverse_total = 1.0 / total
        weight = weight * inverse_total
        latent_weight = latent_weight * inverse_total
        attention[w, 0:tokens, :] = weight
        attention[w, tokens:extent, :] = latent_weight
        weight = weight.astype(bf16)
        latent_weight = latent_weight.astype(bf16)
        attended = dot(weight, values[begin : begin + tokens, :], (0, 0)) + dot(
            latent_weight, latent_values, (0, 0)
        )
        attended = jnp.where(same_head, attended, 0.0)
        parts.append(
            sum(
                attended[h * latent_count : (h + 1) * latent_count, :] for h in range(heads)
            ).astype(bf16)
        )
        where = work * tokens + w * latent_count
        grads[inner : 2 * inner, begin : begin + tokens] = dot(
            wide_grads_t[w], weight, (1, 1)
        ).astype(bf16)
        grads[inner : 2 * inner, where : where + latent_count] = dot(
            wide_grads_t[w], latent_weight, (1, 1)
        ).astype(bf16)
    part = dot(jnp.concatenate(parts, axis=0), out_weight_ref[...]).astype(bf16)
    for w in range(work):
        for m in range(n_mp):
            partial[m, w] = part[
                w * latent_count : (w + 1) * latent_count, m * quarter : (m + 1) * quarter
            ]
    for i in range(4):
        y_copies[i].start()

    def x_copies_of(kind):
        moves = (
            (x_far, top, x_relay.at[kind, 0], dp_right),
            (x_far, bottom, x_relay.at[kind, 1], dp_left),
            (x_right, bottom, x_got.at[kind, 0, bottom], dp_right),
            (x_left, top, x_got.at[kind, 1, top], dp_left),
            (x_right, top, x_got.at[kind, 0, top], dp_right),
            (x_left, bottom, x_got.at[kind, 1, bottom], dp_left),
        )
        return [
            remote(x_sum.at[kind, x, part_rows], dst, x_sems, 6 * kind + i, d, me_m)
            for i, (x, part_rows, dst, d) in enumerate(moves)
        ]

    x_order = (x_far, x_right, x_left, me_x)
    x_copies = [x_copies_of(kind) for kind in range(2)]
    core_copies = [
        [
            remote(
                core_both.at[kind, i, other],
                core_got.at[kind, i],
                core_sems,
                n_x * kind + i,
                dp_other,
                me_m,
            )
            for i in range(n_x)
        ]
        for kind in range(2)
    ]
    inverse = 1.0 / (n_dp * work)

    def join_cores(kind, i):
        core_copies[kind][i].wait_recv()
        x_sum[kind, x_order[i]] = (
            core_both[kind, i, me_core].astype(f32) + core_got[kind, i].astype(f32)
        ).astype(bf16)
        if i == 0:
            x_copies[kind][0].start()
            x_copies[kind][1].start()
        elif i < 3:
            x_copies[kind][i + 1].start()

    def weight_grads(kind):
        for i, x in enumerate(x_order):
            product = dot(grads[kind * inner : (kind + 1) * inner, :], context[x]) * inverse
            for core in range(CORES):
                core_both[kind, i, core] = product[core * half_r : (core + 1) * half_r, :].astype(
                    bf16
                )
            core_copies[kind][i].start()
            if i > 0:
                join_cores(kind, i - 1)

    def relay_x(kind):
        x_copies[kind][0].wait_recv()
        x_sum[kind, x_right, top] = (
            x_sum[kind, x_right, top].astype(f32) + x_relay[kind, 0].astype(f32)
        ).astype(bf16)
        x_copies[kind][4].start()
        x_copies[kind][1].wait_recv()
        x_sum[kind, x_left, bottom] = (
            x_sum[kind, x_left, bottom].astype(f32) + x_relay[kind, 1].astype(f32)
        ).astype(bf16)
        x_copies[kind][5].start()

    def finish_x(kind):
        for i in range(2, 6):
            x_copies[kind][i].wait_recv()
        own = x_sum[kind, me_x].astype(f32)
        return (own + x_got[kind, 0].astype(f32) + x_got[kind, 1].astype(f32)).T

    def key_gradient(w):
        where = work * tokens + w * latent_count
        slope, latent_slope = slopes[w * tokens : (w + 1) * tokens, :], latent_slopes[w]
        weight, latent_weight = attention[w, 0:tokens, :], attention[w, tokens:extent, :]
        row_dot = jnp.sum(weight * slope, axis=0, keepdims=True) + jnp.sum(
            latent_weight * latent_slope, axis=0, keepdims=True
        )
        for begin, count, share_of, slope_of in (
            (w * tokens, tokens, weight, slope),
            (where, latent_count, latent_weight, latent_slope),
        ):
            grad_scores = share_of * (slope_of - row_dot)
            near = grad_scores.astype(bf16)
            rest = (grad_scores - near.astype(f32)).astype(bf16)
            grads[0:inner, begin : begin + count] = (
                (dot(wide_queries_t, near, (1, 1)) + dot(wide_queries_t, rest, (1, 1))) * 0.125
            ).astype(bf16)

    weight_grads(1)
    for w in range(half_w):
        key_gradient(w)
    join_cores(1, n_x - 1)
    y_copies[0].wait_recv()
    y_sum[0] = (partial[y_right, low].astype(f32) + y_relay[0].astype(f32)).astype(bf16)
    y_copies[4].start()
    y_copies[1].wait_recv()
    y_sum[1] = (partial[y_left, high].astype(f32) + y_relay[1].astype(f32)).astype(bf16)
    y_copies[5].start()
    for w in range(half_w, work):
        key_gradient(w)
    relay_x(1)
    weight_grads(0)
    join_cores(0, n_x - 1)
    summed_values = finish_x(1)
    relay_x(0)
    summed_keys = finish_x(0)
    share = quarter // DEPTH
    for z in range(DEPTH):
        its = slice(z * share, (z + 1) * share)
        z_send[z] = jnp.concatenate([summed_keys[its], summed_values[its]], axis=0).astype(bf16)
    z_copies = {
        o: remote(
            z_send.at[z_of(o)],
            z_got.at[o - 1],
            z_sems,
            o - 1,
            at(me_x, z_of(o), me_core),
            me_m,
        )
        for o in range(1, DEPTH)
    }
    for o in sorted(range(1, DEPTH), key=lambda o: -min(o, DEPTH - o)):
        z_copies[o].start()

    for i in range(2, 6):
        y_copies[i].wait_recv()
    mine = latents_ref[:, pl.ds(pl.multiple_of(me_m * quarter, 128), quarter)].astype(f32)
    for w in range(work):
        heads_sum = partial[me_m, w].astype(f32) + y_got[0, w].astype(f32)
        heads_sum = heads_sum + y_got[1, w].astype(f32)
        resampled_ref[w] = ((mine + heads_sum) * alive[w]).astype(bf16)

    total = z_send[me_z].astype(f32)
    for o in sorted(range(1, DEPTH), key=lambda o: min(o, DEPTH - o)):
        z_copies[o].wait_recv()
        total = total + z_got[o - 1].astype(f32)
    last[...] = total
    last_copy = remote(last, last_got, last_sems, 0, dp_other, me_m)
    last_copy.start()
    last_copy.wait_recv()
    first_core = me_core == 0
    ours, theirs = last[...], last_got[...]
    each = share // CORES
    for core, block in enumerate(
        (jnp.where(first_core, ours, theirs), jnp.where(first_core, theirs, ours))
    ):
        for kind, out in enumerate((key_ref, value_ref)):
            piece = block[kind * share : (kind + 1) * share, :]
            out[:, core * 128 : (core + 1) * 128] = jnp.where(
                first_core, piece[:each, :], piece[each:, :]
            )
    started += y_copies + list(z_copies.values()) + [last_copy]
    for kind in range(2):
        started += x_copies[kind] + core_copies[kind]
    for copy in started:
        copy.wait_send()


def hand_over(*refs):
    sources, results, held, sems = refs[:3], refs[3:6], refs[6:9], refs[9]
    taken = [pltpu.make_async_copy(sources[i], held[i], sems.at[0, i]) for i in range(3)]
    given = [pltpu.make_async_copy(held[i], results[i], sems.at[1, i]) for i in range(3)]
    for copy in taken:
        copy.start()
    for first, second in zip(taken, given):
        first.wait()
        second.start()
    for copy in given:
        copy.wait()


def local(
    media,
    time_table,
    doc_images,
    plan,
    latents,
    queries,
    key_weight,
    value_weight,
    out_weight,
    cotangent,
):
    n_dp, n_mp = lax.axis_size("dp"), lax.axis_size("mp")
    slots, tokens, quarter = media.shape
    work, latent_count = cotangent.shape[:2]
    width = latents.shape[1]
    inner = queries.shape[1]
    rows = tokens // CHUNKS
    n_x = n_dp // (DEPTH * CORES)
    share = quarter // DEPTH
    each = inner // CORES
    wide = inner // HEAD * latent_count
    context_rows = work * (tokens + latent_count)
    half = (2, work // 2, latent_count, quarter)
    f32, bf16 = jnp.float32, jnp.bfloat16
    vmem = pl.BlockSpec(memory_space=pltpu.VMEM)
    hbm = pl.BlockSpec(memory_space=pl.ANY)
    dma = pltpu.SemaphoreType.DMA

    def like(x):
        return pltpu.VMEM(x.shape, x.dtype)

    results = pl.pallas_call(
        functools.partial(body, n_dp, n_mp),
        name="resample",
        out_shape=(
            jax.ShapeDtypeStruct((work, latent_count, quarter), bf16),
            jax.ShapeDtypeStruct((share // CORES, inner), f32),
            jax.ShapeDtypeStruct((share // CORES, inner), f32),
        ),
        in_specs=[hbm] * 10,
        out_specs=(vmem,) * 3,
        scratch_shapes=[
            pltpu.SMEM(plan.shape, jnp.int32),
            pltpu.SMEM(doc_images.shape, jnp.int32),
            like(time_table),
            like(media),
            like(queries),
            like(latents),
            like(key_weight),
            like(value_weight),
            like(out_weight),
            pltpu.VMEM((CHUNKS, REACH, rows, quarter), bf16),
            pltpu.VMEM((REACH, 16, quarter), bf16),
            pltpu.VMEM((CHUNKS, REACH, rows, quarter), bf16),
            pltpu.VMEM((REACH, 16, quarter), bf16),
            pltpu.VMEM((n_mp, CHUNKS + 1, work, rows, quarter), bf16),
            pltpu.VMEM((n_mp, context_rows, quarter), bf16),
            pltpu.VMEM((work * latent_count, width), bf16),
            pltpu.VMEM((work * tokens, inner), bf16),
            pltpu.VMEM((work * tokens, wide), f32),
            pltpu.VMEM((work * tokens, wide), f32),
            pltpu.VMEM((work, latent_count, wide), f32),
            pltpu.VMEM((work, wide, inner), bf16),
            pltpu.VMEM((work, inner, wide), bf16),
            pltpu.VMEM((work, tokens + latent_count, wide), f32),
            pltpu.VMEM((2 * inner, context_rows), bf16),
            pltpu.VMEM((n_mp, work, latent_count, quarter), bf16),
            pltpu.VMEM(half, bf16),
            pltpu.VMEM(half, bf16),
            pltpu.VMEM((2, work, latent_count, quarter), bf16),
            pltpu.VMEM((2, n_x, CORES, each, quarter), bf16),
            pltpu.VMEM((2, n_x, each, quarter), bf16),
            pltpu.VMEM((2, n_x, each, quarter), bf16),
            pltpu.VMEM((2, 2, each // 2, quarter), bf16),
            pltpu.VMEM((2, 2, each, quarter), bf16),
            pltpu.VMEM((DEPTH, 2 * share, 128), bf16),
            pltpu.VMEM((DEPTH - 1, 2 * share, 128), bf16),
            pltpu.VMEM((2 * share, 128), f32),
            pltpu.VMEM((2 * share, 128), f32),
            dma((10,)),
            dma((2, CHUNKS * REACH)),
            dma((2, REACH)),
            dma((2, 4 * CHUNKS + 4)),
            dma((2, 6)),
            dma((2, 2 * n_x)),
            dma((2, 12)),
            dma((2, DEPTH - 1)),
            dma((2, 1)),
            pltpu.SemaphoreType.REGULAR((2,)),
        ],
        compiler_params=pltpu.CompilerParams(
            collective_id=0, has_side_effects=True, vmem_limit_bytes=60 << 20
        ),
    )(
        plan,
        doc_images,
        time_table,
        media,
        cotangent,
        queries,
        latents,
        key_weight,
        value_weight,
        out_weight,
    )
    return pl.pallas_call(
        hand_over,
        name="hand_over",
        out_shape=tuple(jax.ShapeDtypeStruct(r.shape, r.dtype) for r in results),
        in_specs=[hbm] * 3,
        out_specs=(hbm,) * 3,
        scratch_shapes=[like(r) for r in results] + [dma((2, 3))],
        compiler_params=pltpu.CompilerParams(vmem_limit_bytes=60 << 20),
    )(*results)


def solution(mesh):
    return jax.shard_map(
        local,
        mesh=mesh,
        in_specs=(
            P("dp", None, "mp"),
            P(None, "mp"),
            P("dp"),
            P("dp", None),
            P(),
            P(None, "mp"),
            P(None, "mp"),
            P(None, "mp"),
            P("mp", None),
            P("dp", None, "mp"),
        ),
        out_specs=(P("dp", None, "mp"), P("dp", "mp"), P("dp", "mp")),
        check_vma=False,
    )
```

```python
import functools

import jax
import jax.numpy as jnp
from jax import lax
from jax.experimental import pallas as pl
from jax.experimental.pallas import tpu as pltpu
from jax.sharding import PartitionSpec as P

HEAD = 64
MESH = pl.DeviceIdType.MESH
CHUNKS = 4
REACH = 4

DEPTH = 16
CORES = 2

norm_epsilon = 1e-05


def plan_scalars(plan_ref, docs_ref, slots, work):
    far_slot = [jnp.int32(0)] * (REACH + 1)
    far_work = [jnp.int32(-1)] * (REACH + 1)
    own_slot = [jnp.int32(0)] * work
    own_live = [jnp.int32(0)] * work
    for s in range(slots):
        code = plan_ref[0, s]
        for k in range(1, REACH + 1):
            inside = (code >= k * work) & (code < (k + 1) * work)
            far_slot[k] = jnp.where(inside, s, far_slot[k])
            far_work[k] = jnp.where(inside, code - k * work, far_work[k])
        for w in range(work):
            own_slot[w] = jnp.where(code == w, s, own_slot[w])
            own_live[w] = jnp.where(code == w, 1, own_live[w])
    first = docs_ref[0]

    def position(s):
        return s - jnp.where(s >= first, first, 0)

    return far_slot, far_work, own_slot, own_live, position


def normalise(parts, width):
    parts = [p.astype(jnp.float32) for p in parts]
    average = sum(jnp.sum(p, axis=-1, keepdims=True) for p in parts) * (1.0 / width)
    parts = [p - average for p in parts]
    spread = sum(jnp.sum(p * p, axis=-1, keepdims=True) for p in parts) * (1.0 / width)
    scale = lax.rsqrt(spread + norm_epsilon)
    return [(p * scale).astype(jnp.bfloat16) for p in parts]


def dot(a, b, dims=(1, 0)):
    return lax.dot_general(
        a, b, (((dims[0],), (dims[1],)), ((), ())), preferred_element_type=jnp.float32
    )


def body(
    n_dp,
    n_mp,
    plan_hbm,
    docs_hbm,
    time_hbm,
    media_hbm,
    cot_hbm,
    queries_hbm,
    latents_hbm,
    key_weight_hbm,
    value_weight_hbm,
    out_weight_hbm,
    resampled_ref,
    key_ref,
    value_ref,
    plan_ref,
    docs_ref,
    time_ref,
    media_ref,
    queries_ref,
    latents_ref,
    key_weight_ref,
    value_weight_ref,
    out_weight_ref,
    send_buf,
    head_buf,
    got_buf,
    got_head,
    full,
    context,
    cot_live,
    values,
    scores,
    slopes,
    latent_slopes,
    wide_grads,
    wide_grads_t,
    attention,
    grads,
    partial,
    y_relay,
    y_sum,
    y_got,
    core_both,
    core_got,
    x_sum,
    x_relay,
    x_got,
    z_send,
    z_got,
    last,
    last_got,
    local_sems,
    far_sems,
    head_sems,
    ring_sems,
    y_sems,
    core_sems,
    x_sems,
    z_sems,
    last_sems,
    known_sems,
):
    f32, bf16 = jnp.float32, jnp.bfloat16
    slots, tokens, quarter = media_hbm.shape
    work, latent_count = cot_hbm.shape[:2]
    width = latents_hbm.shape[1]
    inner = queries_hbm.shape[1]
    heads = inner // HEAD
    rows = tokens // CHUNKS
    half_w = work // 2
    n_x = n_dp // (DEPTH * CORES)
    me_d = lax.axis_index("dp")
    me_m = lax.axis_index("mp")
    me_core = lax.rem(me_d, CORES)
    me_z = lax.rem(me_d // CORES, DEPTH)
    me_x = me_d // (DEPTH * CORES)

    def at(x, z, core):
        return (x * DEPTH + z) * CORES + core

    def far(k):
        return lax.rem(me_d + (k + n_dp), n_dp)

    def z_of(o):
        return lax.rem(me_z + o, DEPTH)

    y_right, y_left = lax.rem(me_m + 1, n_mp), lax.rem(me_m + n_mp - 1, n_mp)
    y_far = lax.rem(me_m + 2, n_mp)
    x_right, x_left = lax.rem(me_x + 1, n_x), lax.rem(me_x + n_x - 1, n_x)
    x_far = lax.rem(me_x + 2, n_x)
    other = 1 - me_core
    dp_right, dp_left = at(x_right, me_z, me_core), at(x_left, me_z, me_core)
    dp_other = at(me_x, me_z, other)

    arguments = [
        (plan_hbm, plan_ref),
        (docs_hbm, docs_ref),
        (time_hbm, time_ref),
    ]
    arguments += [
        (media_hbm, media_ref),
        (cot_hbm, full.at[me_m, CHUNKS]),
        (latents_hbm, latents_ref),
        (key_weight_hbm, key_weight_ref),
        (value_weight_hbm, value_weight_ref),
        (queries_hbm, queries_ref),
        (out_weight_hbm, out_weight_ref),
    ]
    loads = [
        pltpu.make_async_copy(src, dst, local_sems.at[i]) for i, (src, dst) in enumerate(arguments)
    ]
    for load in loads:
        load.start()

    barrier = pltpu.get_barrier_semaphore()
    partners = [(at(me_x, z_of(o), me_core), me_m) for o in (2, DEPTH - 2, 1, DEPTH - 1)]
    for k in range(1, REACH + 1):
        partners += [(far(k), me_m), (far(-k), me_m)]
    partners += [(d, me_m) for d in (dp_right, dp_left, dp_other)]
    partners += [(me_d, y_right), (me_d, y_left)]
    for d, m in partners:
        pl.semaphore_signal(barrier, inc=1, device_id={"dp": d, "mp": m}, device_id_type=MESH)

    for load in loads[:4]:
        load.wait()
    far_slot, far_work, own_slot, own_live, position = plan_scalars(
        plan_ref, docs_ref, slots, work
    )
    times = time_ref[...].astype(f32)
    time_rows = lax.broadcasted_iota(jnp.int32, times.shape, 0)

    def time_of(s):
        return jnp.sum(jnp.where(time_rows == position(s), times, 0.0), axis=0, keepdims=True)

    mark_rows = lax.broadcasted_iota(jnp.int32, head_buf.shape[1:], 0)
    far_rows = [None]
    for k in range(1, REACH + 1):
        head_buf[k - 1] = jnp.where(mark_rows == far_work[k], 1.0, 0.0).astype(bf16)
        far_rows.append(time_of(far_slot[k]))
    own_rows = [time_of(own_slot[w]) for w in range(work)]
    for c in range(CHUNKS):
        for k in range(1, REACH + 1):
            block = media_ref[far_slot[k], c * rows : (c + 1) * rows, :].astype(f32)
            send_buf[c, k - 1] = (block + far_rows[k]).astype(bf16)

    pl.semaphore_wait(barrier, len(partners))

    def greet(i, distance):
        for o in (distance, DEPTH - distance):
            pl.semaphore_signal(
                known_sems.at[i],
                inc=1,
                device_id={"dp": at(me_x, z_of(o), me_core), "mp": me_m},
                device_id_type=MESH,
            )

    greet(0, 2)

    def remote(src, dst, sems, i, d, m):
        return pltpu.make_async_remote_copy(
            src_ref=src,
            dst_ref=dst,
            send_sem=sems.at[0, i],
            recv_sem=sems.at[1, i],
            device_id={"dp": d, "mp": m},
            device_id_type=MESH,
        )

    def own_sends(c, src):
        return [
            remote(src, full.at[me_m, c], ring_sems, 4 * c, me_d, y_right),
            remote(src, full.at[me_m, c], ring_sems, 4 * c + 1, me_d, y_left),
        ]

    def own_arrivals(c):
        return [
            remote(full.at[y_left, c], full.at[y_left, c], ring_sems, 4 * c, me_d, y_right),
            remote(full.at[y_right, c], full.at[y_right, c], ring_sems, 4 * c + 1, me_d, y_left),
        ]

    low, high = pl.ds(0, half_w), pl.ds(half_w, half_w)

    def forwards(c):
        first, second = full.at[y_left, c, low], full.at[y_right, c, high]
        return [
            remote(first, first, ring_sems, 4 * c + 2, me_d, y_right),
            remote(second, second, ring_sems, 4 * c + 3, me_d, y_left),
        ]

    def forward_arrivals(c):
        first, second = full.at[y_far, c, low], full.at[y_far, c, high]
        return [
            remote(first, first, ring_sems, 4 * c + 2, me_d, y_right),
            remote(second, second, ring_sems, 4 * c + 3, me_d, y_left),
        ]

    def far_copy(c, k):
        i = c * REACH + k - 1
        return remote(send_buf.at[c, k - 1], got_buf.at[c, k - 1], far_sems, i, far(k), me_m)

    def head_copy(k):
        return remote(head_buf.at[k - 1], got_head.at[k - 1], head_sems, k - 1, far(k), me_m)

    started = own_sends(CHUNKS, cot_hbm)
    for k in range(REACH, 0, -1):
        started.append(head_copy(k))
    for c in range(CHUNKS):
        for k in range(REACH, 0, -1):
            started.append(far_copy(c, k))
    for copy in started:
        copy.start()

    first_weight = 5
    for load in loads[first_weight - 1 : first_weight + 4]:
        load.wait()
    latent_norm = normalise([latents_ref[...]], width)[0]
    for w in range(work):
        where = work * tokens + w * latent_count
        for m in range(n_mp):
            context[m, where : where + latent_count, :] = latent_norm[
                :, m * quarter : (m + 1) * quarter
            ]
    latent_keys = dot(latent_norm, key_weight_ref[...]).astype(bf16)
    latent_values = dot(latent_norm, value_weight_ref[...]).astype(bf16)
    row_head = lax.broadcasted_iota(jnp.int32, (heads * latent_count, inner), 0) // latent_count
    col_head = lax.broadcasted_iota(jnp.int32, (heads * latent_count, inner), 1) // HEAD
    same_head = row_head == col_head

    def spread_heads(x):
        return jnp.where(same_head, jnp.concatenate([x.astype(f32)] * heads, axis=0), 0.0)

    wide_queries32 = spread_heads(queries_ref[...])
    wide_queries = wide_queries32.astype(bf16)
    wide_queries_t = wide_queries32.T.astype(bf16)
    latent_scores = dot(latent_keys, wide_queries, (1, 1)) * 0.125
    loads[first_weight + 4].wait()

    for k in range(1, REACH + 1):
        head_copy(k).wait_recv()
    marks = [got_head[k].astype(f32) for k in range(REACH)]
    lives = [jnp.where(own_live[w] == 1, 1.0, 0.0) for w in range(work)]
    alive = [sum(marks[k][w : w + 1, :] for k in range(REACH)) + lives[w] for w in range(work)]

    def place(c):
        for k in range(1, REACH + 1):
            far_copy(c, k).wait_recv()
        for w in range(work):
            block = media_ref[own_slot[w], c * rows : (c + 1) * rows, :].astype(f32)
            block = (block + own_rows[w]) * lives[w]
            for k in range(REACH):
                block = block + marks[k][w : w + 1, :] * got_buf[c, k].astype(f32)
            full[me_m, c, w] = block.astype(bf16)
        return own_sends(c, full.at[me_m, c])

    sub = min(32, rows)

    def project(c):
        def norm_rows(i, carry):
            w, r = i // (rows // sub), i % (rows // sub)
            r = pl.multiple_of(r * sub, sub)
            pieces = normalise([full[m, c, w, pl.ds(r, sub), :] for m in range(n_mp)], width)
            where = pl.multiple_of(w * tokens + c * rows + r, sub)
            for m in range(n_mp):
                context[m, pl.ds(where, sub), :] = pieces[m]
            return carry

        lax.fori_loop(0, work * (rows // sub), norm_rows, 0)
        places = [slice(w * tokens + c * rows, w * tokens + (c + 1) * rows) for w in range(work)]
        normed = [
            jnp.concatenate([context[m, p, :] for p in places], axis=0) for m in range(n_mp)
        ]

        def product(weight):
            return sum(
                dot(normed[m], weight[m * quarter : (m + 1) * quarter, :]) for m in range(n_mp)
            ).astype(bf16)

        new_keys, new_values = product(key_weight_ref), product(value_weight_ref)
        new_scores = dot(new_keys, wide_queries, (1, 1)) * 0.125
        for w, p in enumerate(places):
            values[p, :] = new_values[w * rows : (w + 1) * rows, :]
            scores[p, :] = new_scores[w * rows : (w + 1) * rows, :]
            slopes[p, :] = dot(new_values[w * rows : (w + 1) * rows, :], wide_grads[w], (1, 1))

    def pull_back():
        for w in range(work):
            for m in range(n_mp):
                cot_live[
                    w * latent_count : (w + 1) * latent_count, m * quarter : (m + 1) * quarter
                ] = (full[m, CHUNKS, w].astype(f32) * alive[w]).astype(bf16)
        grad_attended = dot(cot_live[...], out_weight_ref[...], (1, 1)).astype(bf16)
        for w in range(work):
            wide = spread_heads(grad_attended[w * latent_count : (w + 1) * latent_count, :])
            wide_grads[w] = wide.astype(bf16)
            wide_grads_t[w] = wide.T.astype(bf16)
            latent_slopes[w] = dot(latent_values, wide.astype(bf16), (1, 1))

    def finish(c):
        for copy in forward_arrivals(c):
            copy.wait_recv()
        if c == CHUNKS:
            pull_back()
        else:
            project(c)

    pl.semaphore_wait(known_sems.at[0], 2)
    greet(1, 4)
    order = [CHUNKS] + list(range(CHUNKS))
    for i, c in enumerate(order):
        if i < CHUNKS:
            copies = place(i)
            for copy in copies:
                copy.start()
            started += copies
        for copy in own_arrivals(c):
            copy.wait_recv()
        copies = forwards(c)
        for copy in copies:
            copy.start()
        started += copies
        if i > 0:
            finish(order[i - 1])
    finish(order[-1])

    half_r = inner // CORES
    top, bottom = pl.ds(0, half_r // 2), pl.ds(half_r // 2, half_r // 2)
    y_copies = [
        remote(partial.at[y_far, low], y_relay.at[0], y_sems, 0, me_d, y_right),
        remote(partial.at[y_far, high], y_relay.at[1], y_sems, 1, me_d, y_left),
        remote(partial.at[y_right, high], y_got.at[0, high], y_sems, 2, me_d, y_right),
        remote(partial.at[y_left, low], y_got.at[1, low], y_sems, 3, me_d, y_left),
        remote(y_sum.at[0], y_got.at[0, low], y_sems, 4, me_d, y_right),
        remote(y_sum.at[1], y_got.at[1, high], y_sems, 5, me_d, y_left),
    ]
    pl.semaphore_wait(known_sems.at[1], 2)
    extent = tokens + latent_count
    parts = []
    for w in range(work):
        begin = w * tokens
        slot_scores = scores[begin : begin + tokens, :]
        top_score = jnp.maximum(
            jnp.max(slot_scores, axis=0, keepdims=True),
            jnp.max(latent_scores, axis=0, keepdims=True),
        )
        weight = jnp.exp(slot_scores - top_score)
        latent_weight = jnp.exp(latent_scores - top_score)
        total = jnp.sum(weight, axis=0, keepdims=True) + jnp.sum(
            latent_weight, axis=0, keepdims=True
        )
        inverse_total = 1.0 / total
        weight = weight * inverse_total
        latent_weight = latent_weight * inverse_total
        attention[w, 0:tokens, :] = weight
        attention[w, tokens:extent, :] = latent_weight
        weight = weight.astype(bf16)
        latent_weight = latent_weight.astype(bf16)
        attended = dot(weight, values[begin : begin + tokens, :], (0, 0)) + dot(
            latent_weight, latent_values, (0, 0)
        )
        attended = jnp.where(same_head, attended, 0.0)
        parts.append(
            sum(
                attended[h * latent_count : (h + 1) * latent_count, :] for h in range(heads)
            ).astype(bf16)
        )
        where = work * tokens + w * latent_count
        grads[inner : 2 * inner, begin : begin + tokens] = dot(
            wide_grads_t[w], weight, (1, 1)
        ).astype(bf16)
        grads[inner : 2 * inner, where : where + latent_count] = dot(
            wide_grads_t[w], latent_weight, (1, 1)
        ).astype(bf16)
    part = dot(jnp.concatenate(parts, axis=0), out_weight_ref[...]).astype(bf16)
    for w in range(work):
        for m in range(n_mp):
            partial[m, w] = part[
                w * latent_count : (w + 1) * latent_count, m * quarter : (m + 1) * quarter
            ]
    for i in range(4):
        y_copies[i].start()

    def x_copies_of(kind):
        moves = (
            (x_far, top, x_relay.at[kind, 0], dp_right),
            (x_far, bottom, x_relay.at[kind, 1], dp_left),
            (x_right, bottom, x_got.at[kind, 0, bottom], dp_right),
            (x_left, top, x_got.at[kind, 1, top], dp_left),
            (x_right, top, x_got.at[kind, 0, top], dp_right),
            (x_left, bottom, x_got.at[kind, 1, bottom], dp_left),
        )
        return [
            remote(x_sum.at[kind, x, part_rows], dst, x_sems, 6 * kind + i, d, me_m)
            for i, (x, part_rows, dst, d) in enumerate(moves)
        ]

    x_order = (x_far, x_right, x_left, me_x)
    x_copies = [x_copies_of(kind) for kind in range(2)]
    core_copies = [
        [
            remote(
                core_both.at[kind, i, other],
                core_got.at[kind, i],
                core_sems,
                n_x * kind + i,
                dp_other,
                me_m,
            )
            for i in range(n_x)
        ]
        for kind in range(2)
    ]
    inverse = 1.0 / (n_dp * work)

    def join_cores(kind, i):
        core_copies[kind][i].wait_recv()
        x_sum[kind, x_order[i]] = (
            core_both[kind, i, me_core].astype(f32) + core_got[kind, i].astype(f32)
        ).astype(bf16)
        if i == 0:
            x_copies[kind][0].start()
            x_copies[kind][1].start()
        elif i < 3:
            x_copies[kind][i + 1].start()

    def weight_grads(kind):
        for i, x in enumerate(x_order):
            product = dot(grads[kind * inner : (kind + 1) * inner, :], context[x]) * inverse
            for core in range(CORES):
                core_both[kind, i, core] = product[core * half_r : (core + 1) * half_r, :].astype(
                    bf16
                )
            core_copies[kind][i].start()
            if i > 0:
                join_cores(kind, i - 1)

    def relay_x(kind):
        x_copies[kind][0].wait_recv()
        x_sum[kind, x_right, top] = (
            x_sum[kind, x_right, top].astype(f32) + x_relay[kind, 0].astype(f32)
        ).astype(bf16)
        x_copies[kind][4].start()
        x_copies[kind][1].wait_recv()
        x_sum[kind, x_left, bottom] = (
            x_sum[kind, x_left, bottom].astype(f32) + x_relay[kind, 1].astype(f32)
        ).astype(bf16)
        x_copies[kind][5].start()

    def finish_x(kind):
        for i in range(2, 6):
            x_copies[kind][i].wait_recv()
        own = x_sum[kind, me_x].astype(f32)
        return (own + x_got[kind, 0].astype(f32) + x_got[kind, 1].astype(f32)).T

    def key_gradient(w):
        where = work * tokens + w * latent_count
        slope, latent_slope = slopes[w * tokens : (w + 1) * tokens, :], latent_slopes[w]
        weight, latent_weight = attention[w, 0:tokens, :], attention[w, tokens:extent, :]
        row_dot = jnp.sum(weight * slope, axis=0, keepdims=True) + jnp.sum(
            latent_weight * latent_slope, axis=0, keepdims=True
        )
        for begin, count, share_of, slope_of in (
            (w * tokens, tokens, weight, slope),
            (where, latent_count, latent_weight, latent_slope),
        ):
            grad_scores = share_of * (slope_of - row_dot)
            near = grad_scores.astype(bf16)
            rest = (grad_scores - near.astype(f32)).astype(bf16)
            grads[0:inner, begin : begin + count] = (
                (dot(wide_queries_t, near, (1, 1)) + dot(wide_queries_t, rest, (1, 1))) * 0.125
            ).astype(bf16)

    weight_grads(1)
    for w in range(half_w):
        key_gradient(w)
    join_cores(1, n_x - 1)
    y_copies[0].wait_recv()
    y_sum[0] = (partial[y_right, low].astype(f32) + y_relay[0].astype(f32)).astype(bf16)
    y_copies[4].start()
    y_copies[1].wait_recv()
    y_sum[1] = (partial[y_left, high].astype(f32) + y_relay[1].astype(f32)).astype(bf16)
    y_copies[5].start()
    for w in range(half_w, work):
        key_gradient(w)
    relay_x(1)
    share = quarter // DEPTH
    far_first = sorted(range(1, DEPTH), key=lambda o: -min(o, DEPTH - o))
    z_copies = [
        {
            o: remote(
                z_send.at[kind, z_of(o)],
                z_got.at[kind, o - 1],
                z_sems,
                kind * (DEPTH - 1) + o - 1,
                at(me_x, z_of(o), me_core),
                me_m,
            )
            for o in range(1, DEPTH)
        }
        for kind in range(2)
    ]

    def start_z(kind):
        summed = finish_x(kind)
        for z in range(DEPTH):
            z_send[kind, z] = summed[z * share : (z + 1) * share, :].astype(bf16)
        for o in far_first:
            z_copies[kind][o].start()

    weight_grads(0)
    start_z(1)
    relay_x(0)
    join_cores(0, n_x - 1)
    start_z(0)

    for kind in (1, 0):
        total = z_send[kind, me_z].astype(f32)
        for o in reversed(far_first):
            z_copies[kind][o].wait_recv()
            total = total + z_got[kind, o - 1].astype(f32)
        last[kind * share : (kind + 1) * share, :] = total
    last_copy = remote(last, last_got, last_sems, 0, dp_other, me_m)
    last_copy.start()

    for i in range(2, 6):
        y_copies[i].wait_recv()
    mine = latents_ref[:, pl.ds(pl.multiple_of(me_m * quarter, 128), quarter)].astype(f32)
    for w in range(work):
        heads_sum = partial[me_m, w].astype(f32) + y_got[0, w].astype(f32)
        heads_sum = heads_sum + y_got[1, w].astype(f32)
        resampled_ref[w] = ((mine + heads_sum) * alive[w]).astype(bf16)

    last_copy.wait_recv()
    first_core = me_core == 0
    ours, theirs = last[...], last_got[...]
    each = share // CORES
    for core, block in enumerate(
        (jnp.where(first_core, ours, theirs), jnp.where(first_core, theirs, ours))
    ):
        for kind, out in enumerate((key_ref, value_ref)):
            piece = block[kind * share : (kind + 1) * share, :]
            out[:, core * 128 : (core + 1) * 128] = jnp.where(
                first_core, piece[:each, :], piece[each:, :]
            )
    started += y_copies + [last_copy]
    for kind in range(2):
        started += x_copies[kind] + core_copies[kind] + list(z_copies[kind].values())
    for copy in started:
        copy.wait_send()


def hand_over(*refs):
    sources, results, held, sems = refs[:3], refs[3:6], refs[6:9], refs[9]
    taken = [pltpu.make_async_copy(sources[i], held[i], sems.at[0, i]) for i in range(3)]
    given = [pltpu.make_async_copy(held[i], results[i], sems.at[1, i]) for i in range(3)]
    for copy in taken:
        copy.start()
    for first, second in zip(taken, given):
        first.wait()
        second.start()
    for copy in given:
        copy.wait()


def local(
    media,
    time_table,
    doc_images,
    plan,
    latents,
    queries,
    key_weight,
    value_weight,
    out_weight,
    cotangent,
):
    n_dp, n_mp = lax.axis_size("dp"), lax.axis_size("mp")
    slots, tokens, quarter = media.shape
    work, latent_count = cotangent.shape[:2]
    width = latents.shape[1]
    inner = queries.shape[1]
    rows = tokens // CHUNKS
    n_x = n_dp // (DEPTH * CORES)
    share = quarter // DEPTH
    each = inner // CORES
    wide = inner // HEAD * latent_count
    context_rows = work * (tokens + latent_count)
    half = (2, work // 2, latent_count, quarter)
    f32, bf16 = jnp.float32, jnp.bfloat16
    vmem = pl.BlockSpec(memory_space=pltpu.VMEM)
    hbm = pl.BlockSpec(memory_space=pl.ANY)
    dma = pltpu.SemaphoreType.DMA

    def like(x):
        return pltpu.VMEM(x.shape, x.dtype)

    results = pl.pallas_call(
        functools.partial(body, n_dp, n_mp),
        name="resample",
        out_shape=(
            jax.ShapeDtypeStruct((work, latent_count, quarter), bf16),
            jax.ShapeDtypeStruct((share // CORES, inner), f32),
            jax.ShapeDtypeStruct((share // CORES, inner), f32),
        ),
        in_specs=[hbm] * 10,
        out_specs=(vmem,) * 3,
        scratch_shapes=[
            pltpu.SMEM(plan.shape, jnp.int32),
            pltpu.SMEM(doc_images.shape, jnp.int32),
            like(time_table),
            like(media),
            like(queries),
            like(latents),
            like(key_weight),
            like(value_weight),
            like(out_weight),
            pltpu.VMEM((CHUNKS, REACH, rows, quarter), bf16),
            pltpu.VMEM((REACH, 16, quarter), bf16),
            pltpu.VMEM((CHUNKS, REACH, rows, quarter), bf16),
            pltpu.VMEM((REACH, 16, quarter), bf16),
            pltpu.VMEM((n_mp, CHUNKS + 1, work, rows, quarter), bf16),
            pltpu.VMEM((n_mp, context_rows, quarter), bf16),
            pltpu.VMEM((work * latent_count, width), bf16),
            pltpu.VMEM((work * tokens, inner), bf16),
            pltpu.VMEM((work * tokens, wide), f32),
            pltpu.VMEM((work * tokens, wide), f32),
            pltpu.VMEM((work, latent_count, wide), f32),
            pltpu.VMEM((work, wide, inner), bf16),
            pltpu.VMEM((work, inner, wide), bf16),
            pltpu.VMEM((work, tokens + latent_count, wide), f32),
            pltpu.VMEM((2 * inner, context_rows), bf16),
            pltpu.VMEM((n_mp, work, latent_count, quarter), bf16),
            pltpu.VMEM(half, bf16),
            pltpu.VMEM(half, bf16),
            pltpu.VMEM((2, work, latent_count, quarter), bf16),
            pltpu.VMEM((2, n_x, CORES, each, quarter), bf16),
            pltpu.VMEM((2, n_x, each, quarter), bf16),
            pltpu.VMEM((2, n_x, each, quarter), bf16),
            pltpu.VMEM((2, 2, each // 2, quarter), bf16),
            pltpu.VMEM((2, 2, each, quarter), bf16),
            pltpu.VMEM((2, DEPTH, share, 128), bf16),
            pltpu.VMEM((2, DEPTH - 1, share, 128), bf16),
            pltpu.VMEM((2 * share, 128), f32),
            pltpu.VMEM((2 * share, 128), f32),
            dma((10,)),
            dma((2, CHUNKS * REACH)),
            dma((2, REACH)),
            dma((2, 4 * CHUNKS + 4)),
            dma((2, 6)),
            dma((2, 2 * n_x)),
            dma((2, 12)),
            dma((2, 2 * DEPTH - 2)),
            dma((2, 1)),
            pltpu.SemaphoreType.REGULAR((2,)),
        ],
        compiler_params=pltpu.CompilerParams(
            collective_id=0, has_side_effects=True, vmem_limit_bytes=60 << 20
        ),
    )(
        plan,
        doc_images,
        time_table,
        media,
        cotangent,
        queries,
        latents,
        key_weight,
        value_weight,
        out_weight,
    )
    return pl.pallas_call(
        hand_over,
        name="hand_over",
        out_shape=tuple(jax.ShapeDtypeStruct(r.shape, r.dtype) for r in results),
        in_specs=[hbm] * 3,
        out_specs=(hbm,) * 3,
        scratch_shapes=[like(r) for r in results] + [dma((2, 3))],
        compiler_params=pltpu.CompilerParams(vmem_limit_bytes=60 << 20),
    )(*results)


def solution(mesh):
    return jax.shard_map(
        local,
        mesh=mesh,
        in_specs=(
            P("dp", None, "mp"),
            P(None, "mp"),
            P("dp"),
            P("dp", None),
            P(),
            P(None, "mp"),
            P(None, "mp"),
            P(None, "mp"),
            P("mp", None),
            P("dp", None, "mp"),
        ),
        out_specs=(P("dp", None, "mp"), P("dp", "mp"), P("dp", "mp")),
        check_vma=False,
    )
```
